256 devices in a mesh: wall: 16 (over y, x), stream: 16 (over z, core).
Axes of the slice: x: 4, y: 4, z: 8, core: 2. Of those that a mesh axis runs over, the one named last changes fastest.
Arguments:
- residual_rhs: float32 [128, 16, 2048], P('wall', None, 'stream'), may hold values from -6 to 6
- pivot_inverse: bfloat16 [128, 16, 16, 2048], P('wall', None, None, 'stream'), may hold values from -0.3125 to 0.3125
- lower_factor: bfloat16 [128, 16, 16, 2048], P('wall', None, None, 'stream'), may hold values from -1 to 1
- upper_factor: bfloat16 [128, 16, 16, 2048], P('wall', None, None, 'stream'), may hold values from -1 to 1
- west_jacobian: bfloat16 [128, 16, 16, 2048], P('wall', None, None, 'stream'), may hold values from -0.1875 to 0.1875
- east_jacobian: bfloat16 [128, 16, 16, 2048], P('wall', None, None, 'stream'), may hold values from -0.1875 to 0.1875
- species_mask: int32 [16, 16], replicated, may hold values 0 or 1
- cell_codes: int32 [128, 2048], P('wall', 'stream'), may hold values from 0 to 3
Outputs:
- update: float32 [128, 16, 2048], P('wall', None, 'stream')
The draws below stay inside these ranges and needn't reach their ends.
All inputs are finite; a program needn't handle non-finite values.
Results may differ from the reference program's by a relative error of at most 0.0003.
Values sent between devices are 32-bit elements; how exact they have to be, the bound alone decides.
A program may use at most 64 MiB of HBM per device.

```python
import jax
import jax.numpy as jnp
from jax import lax

CELL_EQUATIONS = 16
SWEEPS = 3
CW = 8
WALL_CELLS = 128
STREAM_CELLS = 2048


def chain_factor(seed_key):
    child_key_list = jax.random.split(seed_key, 8)
    picked = jax.random.uniform(child_key_list[0], (CELL_EQUATIONS,))
    slow_share = 0.5
    slow_rows = picked < slow_share
    group_label = jax.random.randint(child_key_list[7], (CELL_EQUATIONS,), 0, 4)
    same_group = group_label[:, None] == group_label[None, :]
    cell_wall_position = jnp.arange(WALL_CELLS)
    factor_two = 1.0 + (cell_wall_position // CW % 2).astype(jnp.float32)
    base_rate = jax.random.uniform(child_key_list[1], (CELL_EQUATIONS,), minval=0.25, maxval=0.75) / WALL_CELLS
    sluggish_rate = 1.0 - base_rate[None, :, None] * factor_two[:, None, None]
    fast_rate = jax.random.uniform(child_key_list[2], (WALL_CELLS, CELL_EQUATIONS, STREAM_CELLS), minval=0.92, maxval=0.95)
    sudden_cells = jax.random.randint(child_key_list[3], (3,), 0, WALL_CELLS)
    sudden_flagged = jnp.any(cell_wall_position[:, None] == sudden_cells[None, :], axis=1)
    sudden_threshold = jax.random.uniform(child_key_list[4], (WALL_CELLS, CELL_EQUATIONS, STREAM_CELLS), minval=0.5, maxval=0.8)
    sluggish_complete = sluggish_rate * jnp.where(sudden_flagged[:, None, None], sudden_threshold, 1.0)
    row_rate = jnp.where(slow_rows[None, :, None], sluggish_complete, fast_rate)
    slow_partner = slow_rows[None, :] & same_group
    allowed = jnp.where(slow_rows[:, None], slow_partner, True) & jnp.logical_not(jnp.eye(CELL_EQUATIONS, dtype=bool))
    allowed_f = allowed.astype(jnp.float32)
    per_row = jnp.maximum(jnp.sum(allowed_f, axis=1), 1.0)
    spread = jax.random.uniform(child_key_list[5], (WALL_CELLS, CELL_EQUATIONS, CELL_EQUATIONS, STREAM_CELLS))
    off_part = spread * (allowed_f / per_row[:, None] * 0.4)[None, :, :, None] * row_rate[:, :, None, :]
    diag_part = row_rate - jnp.sum(off_part, axis=2)
    signs = jnp.where(jax.random.uniform(child_key_list[6], (WALL_CELLS, 1, 1, STREAM_CELLS)) < 0.5, -1.0, 1.0)
    full = signs * (off_part + jnp.eye(CELL_EQUATIONS, dtype=jnp.float32)[None, :, :, None] * diag_part[:, :, None, :])
    return full.astype(jnp.bfloat16)


def draw_lower_factor(key, part):
    return chain_factor(jax.random.fold_in(key, 11))


def draw_upper_factor(key, part):
    return chain_factor(jax.random.fold_in(key, 23))


def place_ends(values, key, low, largest):
    spot = [jax.random.randint(jax.random.fold_in(key, axis), (), 0, length) for axis, length in enumerate(values.shape)]
    widest = values.shape.index(max(values.shape))
    beside = spot[:widest] + [(spot[widest] + 1) % values.shape[widest]] + spot[widest + 1:]
    return values.at[tuple(spot)].set(low).at[tuple(beside)].set(largest)


def block_scale(key, dims, cuts, low, largest):
    factor_of, own = 1.0, jax.random.fold_in(key, 6)
    for position, blocks in cuts:
        steps = jnp.exp(jax.random.uniform(jax.random.fold_in(own, position), (blocks,), jnp.float32, low / len(cuts), largest / len(cuts)))
        factor_of = factor_of * jnp.repeat(steps, dims[position] // blocks).reshape([-1 if axis == position else 1 for axis in range(len(dims))])
    return factor_of


def noise(key, extent, scale, bound, shards=(), kind=jnp.bfloat16):
    entries = scale * jax.random.normal(key, extent, jnp.float32)
    if shards:
        entries = entries * block_scale(key, extent, shards, -0.22, 0.18)
    return jnp.clip(entries, -bound, bound).astype(kind)


def setup_inputs(seed: int = 0) -> dict:
    key_list = jax.random.split(jax.random.key(seed), 9)
    residual_rhs = noise(key_list[0], (WALL_CELLS, CELL_EQUATIONS, STREAM_CELLS), 1.0, 6.0, ((0, 16), (2, 16)), jnp.float32)
    pivot_inverse = noise(key_list[1], (WALL_CELLS, CELL_EQUATIONS, CELL_EQUATIONS, STREAM_CELLS), 400 ** -0.5, 0.3125, ((0, 16), (3, 16)))
    lower_factor = draw_lower_factor(jax.random.fold_in(key_list[8], 71), 0)
    upper_factor = draw_upper_factor(jax.random.fold_in(key_list[8], 71), 0)
    west_jacobian = noise(key_list[4], (WALL_CELLS, CELL_EQUATIONS, CELL_EQUATIONS, STREAM_CELLS), 1024 ** -0.5, 0.1875, ((0, 16), (3, 16)))
    east_jacobian = noise(key_list[5], (WALL_CELLS, CELL_EQUATIONS, CELL_EQUATIONS, STREAM_CELLS), 1024 ** -0.5, 0.1875, ((0, 16), (3, 16)))
    species_mask = place_ends((jax.random.randint(key_list[6], (CELL_EQUATIONS, CELL_EQUATIONS), 0, 4) < 3).astype(jnp.int32), jax.random.fold_in(key_list[6], 1), 0, 1)
    cell_codes = place_ends(jax.random.randint(key_list[7], (WALL_CELLS, STREAM_CELLS), 0, 4), jax.random.fold_in(key_list[7], 1), 0, 3).astype(jnp.int32)
    return dict(residual_rhs=residual_rhs, pivot_inverse=pivot_inverse, lower_factor=lower_factor, upper_factor=upper_factor, west_jacobian=west_jacobian, east_jacobian=east_jacobian, species_mask=species_mask, cell_codes=cell_codes)


def multiply_cells(blocks, vectors):
    return jnp.einsum("wcks,wks->wcs", blocks.astype(jnp.float32), vectors, precision=lax.Precision.HIGHEST)


def chain_sweep(factor, source, reverse):
    def advance(current, inputs):
        factor_cell, source_cell = inputs
        summed = jnp.einsum("cks,ks->cs", factor_cell.astype(jnp.float32), current, precision=lax.Precision.HIGHEST)
        current = source_cell + summed
        return current, current

    start = jnp.zeros(source.shape[1:], jnp.float32)
    _, result = lax.scan(advance, start, (factor, source), reverse=reverse)
    return result


def reference(residual_rhs, pivot_inverse, lower_factor, upper_factor, west_jacobian, east_jacobian, species_mask, cell_codes):
    mask_bf = species_mask.astype(jnp.bfloat16)[None, :, :, None]
    west_masked = west_jacobian * mask_bf
    east_masked = east_jacobian * mask_bf
    west_on = ((cell_codes == 0) | (cell_codes == 1)).astype(jnp.float32)[:, None, :]
    east_on = ((cell_codes == 0) | (cell_codes == 2)).astype(jnp.float32)[:, None, :]
    update = jnp.zeros(residual_rhs.shape, jnp.float32)
    for sweep_index in range(SWEEPS):
        padded = jnp.pad(update, ((0, 0), (0, 0), (1, 1)))
        source = residual_rhs - west_on * multiply_cells(west_masked, padded[:, :, :-2])
        source = source - east_on * multiply_cells(east_masked, padded[:, :, 2:])
        forward = multiply_cells(pivot_inverse, source)
        lines = chain_sweep(lower_factor, forward, False)
        update = chain_sweep(upper_factor, lines, True)
    return update
```

```python
import jax
import jax.numpy as jnp
from jax import lax
from jax.experimental import pallas as pl
from jax.experimental.pallas import tpu as pltpu
from jax.sharding import PartitionSpec as P

SWEEPS = 3
EQ = 16
CELLS = 8
LANES = 128
WALL = 16
SIDE = 4
BLOCK = EQ * EQ
MESH = pl.DeviceIdType.MESH
F32 = jnp.float32

OFFSETS = sorted(
    [(dy, dx) for dy in range(SIDE) for dx in range(SIDE) if dy or dx],
    key=lambda o: -(min(o[0], SIDE - o[0]) + min(o[1], SIDE - o[1])),
)


def rows(start, size):
    return pl.ds(start, size)


def tree_sum(parts):
    while len(parts) > 1:
        parts = [
            parts[k] + parts[k + 1] if k + 1 < len(parts) else parts[k]
            for k in range(0, len(parts), 2)
        ]
    return parts[0]


def times(blocks, base, vectors, at):
    return tree_sum(
        [
            blocks[rows(base + EQ * k, EQ), :] * vectors[rows(at + k, 1), :]
            for k in range(EQ)
        ]
    )


def block_product(out, out_base, left, left_base, right, right_base, add=None, add_base=0):
    def some_columns(step, carry):
        first = pl.multiple_of(step * (4 * EQ), 4 * EQ)
        sums = [None] * 4
        if add is not None:
            sums = [add[rows(add_base + first + EQ * m, EQ), :] for m in range(4)]
        for k in range(EQ):
            column = left[rows(left_base + EQ * k, EQ), :]
            for m in range(4):
                term = column * right[rows(right_base + first + EQ * m + k, 1), :]
                sums[m] = term if sums[m] is None else sums[m] + term
        for m in range(4):
            out[rows(out_base + first + EQ * m, EQ), :] = sums[m]
        return carry

    lax.fori_loop(0, 4, some_columns, 0)


def swap_blocks(values, lane):
    count = len(values)
    width = LANES // count
    half = count // 2
    while half >= 1:
        distance = half * width
        upper = (lane & distance) != 0
        moved = list(values)
        for v in range(count):
            if v & half == 0:
                low, high = values[v], values[v + half]
                moved[v] = jnp.where(upper, pltpu.roll(high, distance, 1), low)
                moved[v + half] = jnp.where(upper, high, pltpu.roll(low, LANES - distance, 1))
        values = moved
        half //= 2
    return values


def kernel(
    rhs, pivot_in, lower_in, upper_in, west_in, east_in, mask_in, codes, out,
    temp, mask_cols, pivot, lower, upper, west, east,
    c_maps, d_maps, b_maps, p_pack, d_pack, b_pack,
    f_rows, q_rows, r_rows, u_rows, uw_rows, ue_rows, s_rows, ab_rows, solve_rows,
    map_out, map_in, vec_out, vec_in, halo_out, halo_in,
    map_send, map_recv, vec_send, vec_recv, halo_send, halo_recv,
):
    me = lax.axis_index("wall")
    stream = lax.axis_index("stream")
    streams = lax.axis_size("stream")
    my_y, my_x = me // SIDE, me % SIDE
    peers = [((my_y + dy) % SIDE) * SIDE + (my_x + dx) % SIDE for dy, dx in OFFSETS]
    next_stream = lax.rem(stream + 1, streams)
    last_stream = lax.rem(stream + streams - 1, streams)
    lane = lax.broadcasted_iota(jnp.int32, (8, LANES), 1)
    lane16 = lax.broadcasted_iota(jnp.int32, (EQ, LANES), 1)

    barrier = pltpu.get_barrier_semaphore()
    for peer in peers:
        pl.semaphore_signal(barrier, inc=1, device_id={"wall": peer}, device_id_type=MESH)
    for other in (next_stream, last_stream):
        pl.semaphore_signal(barrier, inc=1, device_id={"stream": other}, device_id_type=MESH)

    def by_columns(source, target, scale=None):
        def one_cell(j, carry):
            base = pl.multiple_of(j * BLOCK, BLOCK)
            for c in range(EQ):
                temp[rows(base + EQ * c, EQ), :] = source[j, c].astype(F32)
            factor = None if scale is None else scale(j)
            for k in range(EQ):
                column = temp[pl.ds(base + k, EQ, stride=EQ), :]
                if factor is not None:
                    column = column * (mask_cols[EQ * k : EQ * k + EQ, :] * factor)
                target[rows(base + EQ * k, EQ), :] = column
            return carry

        lax.fori_loop(0, CELLS, one_cell, 0)

    by_columns(pivot_in, pivot)
    by_columns(lower_in, lower)
    by_columns(upper_in, upper)

    def forward_cell(j, carry):
        base = pl.multiple_of(j * BLOCK, BLOCK)
        at = pl.multiple_of(j * EQ, EQ)
        f_rows[rows(at, EQ), :] = times(pivot, base, s_rows, at)
        return carry

    def local_chains():
        q_rows[0:EQ, :] = f_rows[0:EQ, :]

        def up(j, carry):
            base = pl.multiple_of(j * BLOCK, BLOCK)
            at = pl.multiple_of(j * EQ, EQ)
            q_rows[rows(at, EQ), :] = f_rows[rows(at, EQ), :] + times(lower, base, q_rows, at - EQ)
            return carry

        lax.fori_loop(1, CELLS, up, 0)
        last = (CELLS - 1) * EQ
        r_rows[last : last + EQ, :] = q_rows[last : last + EQ, :]

        def down(step, carry):
            j = CELLS - 1 - step
            base = pl.multiple_of(j * BLOCK, BLOCK)
            at = pl.multiple_of(j * EQ, EQ)
            r_rows[rows(at, EQ), :] = q_rows[rows(at, EQ), :] + times(upper, base, r_rows, at + EQ)
            return carry

        lax.fori_loop(1, CELLS, down, 0)

    def vec_copy(turn, peer):
        return pltpu.make_async_remote_copy(
            src_ref=vec_out.at[turn, peer // SIDE],
            dst_ref=vec_in.at[turn, me],
            send_sem=vec_send.at[turn, peer],
            recv_sem=vec_recv.at[turn, me],
            device_id={"wall": peer},
            device_id_type=MESH,
        )

    def vec_arrival(turn, peer):
        return pltpu.make_async_remote_copy(
            src_ref=vec_out.at[turn, 0],
            dst_ref=vec_in.at[turn, peer],
            send_sem=vec_send.at[turn, peer],
            recv_sem=vec_recv.at[turn, peer],
            device_id={"wall": peer},
            device_id_type=MESH,
        )

    def send_vectors(turn, values):
        for u, value in enumerate(swap_blocks(values, lane)):
            vec_out[turn, u] = value
        for peer in peers:
            vec_copy(turn, peer).start()
        vec_in[turn, me] = vec_out[turn, my_y]

    def take_vectors(turn):
        for peer in peers:
            vec_arrival(turn, peer).wait_recv()
        for peer in peers:
            vec_copy(turn, peer).wait_send()
        gathered = []
        slot = (lane // 8) % SIDE
        for high in range(SIDE):
            chosen = None
            for low in range(SIDE):
                shift = (8 * (low - my_x) + LANES) % LANES
                piece = pltpu.roll(vec_in[turn, SIDE * high + low], shift, 1)
                chosen = piece if chosen is None else jnp.where(slot == low, piece, chosen)
            gathered.append(chosen)
        return swap_blocks(gathered, lane)

    def map_copy(which, peer):
        return pltpu.make_async_remote_copy(
            src_ref=map_out.at[which, peer],
            dst_ref=map_in.at[which, me],
            send_sem=map_send.at[which, peer],
            recv_sem=map_recv.at[which, me],
            device_id={"wall": peer},
            device_id_type=MESH,
        )

    def map_arrival(which, peer):
        return pltpu.make_async_remote_copy(
            src_ref=map_out.at[which, peer],
            dst_ref=map_in.at[which, peer],
            send_sem=map_send.at[which, peer],
            recv_sem=map_recv.at[which, peer],
            device_id={"wall": peer},
            device_id_type=MESH,
        )

    def send_map(which, maps, base):
        def one_half(half, carry):
            at = pl.multiple_of(half * 8, 8)
            values = [maps[rows(base + EQ * m + at, 8), :] for m in range(EQ)]
            for g, value in enumerate(swap_blocks(values, lane)):
                map_out[which, g, rows(at, 8), :] = value
            return carry

        lax.fori_loop(0, 2, one_half, 0)
        for peer in peers:
            map_copy(which, peer).start()
        map_in[which, me] = map_out[which, me]

    def take_map(which, packed, keep):
        for peer in peers:
            map_arrival(which, peer).wait_recv()
        for peer in peers:
            map_copy(which, peer).wait_send()

        def one_half(half, carry):
            at = pl.multiple_of(half * 8, 8)
            values = [map_in[which, i, rows(at, 8), :] for i in range(WALL)]
            for m, value in enumerate(swap_blocks(values, lane)):
                if keep is not None:
                    value = jnp.where(keep, value, 0.0)
                packed[rows(EQ * m + at, 8), :] = value
            return carry

        lax.fori_loop(0, 2, one_half, 0)

    for j in range(CELLS):
        s_rows[EQ * j : EQ * j + EQ, :] = rhs[j]
    lax.fori_loop(0, CELLS, forward_cell, 0)
    local_chains()
    top = (CELLS - 1) * EQ

    def edge_vectors():
        return [
            q_rows[top : top + 8, :],
            q_rows[top + 8 : top + 16, :],
            r_rows[0:8, :],
            r_rows[8:16, :],
        ]

    pl.semaphore_wait(barrier, len(peers) + 2)
    send_vectors(0, edge_vectors())

    c_maps[0:BLOCK, :] = lower[0:BLOCK, :]
    d_maps[(CELLS - 1) * BLOCK : CELLS * BLOCK, :] = upper[(CELLS - 1) * BLOCK : CELLS * BLOCK, :]

    def c_cell(j, carry):
        base = pl.multiple_of(j * BLOCK, BLOCK)
        block_product(c_maps, base, lower, base, c_maps, base - BLOCK)
        return carry

    lax.fori_loop(1, CELLS, c_cell, 0)
    send_map(0, c_maps, (CELLS - 1) * BLOCK)

    def d_cell(step, carry):
        base = pl.multiple_of((CELLS - 1 - step) * BLOCK, BLOCK)
        block_product(d_maps, base, upper, base, d_maps, base + BLOCK)
        return carry

    lax.fori_loop(1, CELLS, d_cell, 0)
    send_map(1, d_maps, 0)
    final = (CELLS - 1) * BLOCK
    b_maps[final : final + BLOCK, :] = c_maps[final : final + BLOCK, :]

    def b_cell(step, carry):
        base = pl.multiple_of((CELLS - 1 - step) * BLOCK, BLOCK)
        block_product(b_maps, base, upper, base, b_maps, base + BLOCK, c_maps, base)
        return carry

    lax.fori_loop(1, CELLS, b_cell, 0)
    send_map(2, b_maps, 0)

    for k in range(EQ):
        column = mask_in[:, k : k + 1].astype(F32)
        mask_cols[EQ * k : EQ * k + EQ, :] = jnp.broadcast_to(column, (EQ, LANES))

    def west_on(j):
        code = codes[rows(j, 1), :]
        return jnp.where((code == 0) | (code == 1), 1.0, 0.0).astype(F32)

    def east_on(j):
        code = codes[rows(j, 1), :]
        return jnp.where((code == 0) | (code == 2), 1.0, 0.0).astype(F32)

    by_columns(west_in, west, west_on)
    by_columns(east_in, east, east_on)

    first_group = lane < 8
    take_map(0, p_pack, jnp.logical_not(first_group))
    take_map(1, d_pack, lane < LANES - 8)
    take_map(2, b_pack, jnp.logical_not(first_group))

    def halo_copy(sweep, side, other):
        return pltpu.make_async_remote_copy(
            src_ref=halo_out.at[sweep, side],
            dst_ref=halo_in.at[sweep, side],
            send_sem=halo_send.at[sweep, side],
            recv_sem=halo_recv.at[sweep, side],
            device_id={"stream": other},
            device_id_type=MESH,
        )

    def one_sweep(sweep, carry):
        q_low, q_high, r_low, r_high = take_vectors(0)

        solve_rows[0:8, :] = pltpu.roll(q_low, 8, 1)
        solve_rows[8:16, :] = pltpu.roll(q_high, 8, 1)
        q_all = jnp.concatenate([q_low, q_high], axis=0)
        r_all = jnp.concatenate([r_low, r_high], axis=0)

        def rise(step, carry):
            outflow = q_all + times(p_pack, 0, solve_rows, 0)
            solve_rows[0:EQ, :] = pltpu.roll(outflow, 8, 1)
            return carry

        lax.fori_loop(0, WALL - 2, rise, 0)
        down_all = r_all + times(b_pack, 0, solve_rows, 0)
        solve_rows[EQ : 2 * EQ, :] = pltpu.roll(down_all, LANES - 8, 1)

        def fall(step, carry):
            outflow = down_all + times(d_pack, 0, solve_rows, EQ)
            solve_rows[EQ : 2 * EQ, :] = pltpu.roll(outflow, LANES - 8, 1)
            return carry

        lax.fori_loop(0, WALL - 2, fall, 0)
        a_all = jnp.where(lane16 < 8, 0.0, solve_rows[0:EQ, :])
        b_all = jnp.where(lane16 < LANES - 8, solve_rows[EQ : 2 * EQ, :], 0.0)
        send_vectors(1, [a_all[0:8], a_all[8:16], b_all[0:8], b_all[8:16]])
        for v, value in enumerate(take_vectors(1)):
            ab_rows[8 * v : 8 * v + 8, :] = value

        def update_cell(j, carry):
            base = pl.multiple_of(j * BLOCK, BLOCK)
            at = pl.multiple_of(j * EQ, EQ)
            u_rows[rows(at, EQ), :] = (
                r_rows[rows(at, EQ), :]
                + times(b_maps, base, ab_rows, 0)
                + times(d_maps, base, ab_rows, EQ)
            )
            return carry

        lax.fori_loop(0, CELLS, update_cell, 0)

        @pl.when(sweep < SWEEPS - 1)
        def _():
            to_east = jnp.zeros((EQ, LANES), F32)
            to_west = jnp.zeros((EQ, LANES), F32)
            for j in range(CELLS):
                value = u_rows[EQ * j : EQ * j + EQ, :]
                to_east = jnp.where(lane16 == j, pltpu.roll(value, j + 1, 1), to_east)
                to_west = jnp.where(lane16 == j, pltpu.roll(value, j, 1) if j else value, to_west)
            halo_out[sweep, 0] = to_east
            halo_out[sweep, 1] = to_west
            halo_copy(sweep, 0, next_stream).start()
            halo_copy(sweep, 1, last_stream).start()
            halo_copy(sweep, 0, next_stream).wait()
            halo_copy(sweep, 1, last_stream).wait()
            from_west = jnp.where(stream == 0, 0.0, halo_in[sweep, 0])
            from_east = jnp.where(stream == streams - 1, 0.0, halo_in[sweep, 1])
            for j in range(CELLS):
                value = u_rows[EQ * j : EQ * j + EQ, :]
                ghost = pltpu.roll(from_west, LANES - j, 1) if j else from_west
                uw_rows[EQ * j : EQ * j + EQ, :] = jnp.where(
                    lane16 == 0, ghost, pltpu.roll(value, 1, 1)
                )
                ghost = pltpu.roll(from_east, LANES - 1 - j, 1)
                ue_rows[EQ * j : EQ * j + EQ, :] = jnp.where(
                    lane16 == LANES - 1, ghost, pltpu.roll(value, LANES - 1, 1)
                )

            def source_cell(j, carry):
                base = pl.multiple_of(j * BLOCK, BLOCK)
                at = pl.multiple_of(j * EQ, EQ)
                s_rows[rows(at, EQ), :] = (
                    rhs[j] - times(west, base, uw_rows, at) - times(east, base, ue_rows, at)
                )
                return carry

            lax.fori_loop(0, CELLS, source_cell, 0)
            lax.fori_loop(0, CELLS, forward_cell, 0)
            local_chains()
            send_vectors(0, edge_vectors())

        return carry

    lax.fori_loop(0, SWEEPS, one_sweep, 0)
    for j in range(CELLS):
        out[j] = u_rows[EQ * j : EQ * j + EQ, :]


def on_device(*arrays):
    big = pltpu.VMEM((CELLS * BLOCK, LANES), F32)
    block = pltpu.VMEM((BLOCK, LANES), F32)
    vectors = pltpu.VMEM((CELLS * EQ, LANES), F32)
    pair = pltpu.VMEM((2 * EQ, LANES), F32)
    return pl.pallas_call(
        kernel,
        out_shape=jax.ShapeDtypeStruct((CELLS, EQ, LANES), F32),
        in_specs=[pl.BlockSpec(memory_space=pltpu.VMEM)] * 8,
        out_specs=pl.BlockSpec(memory_space=pltpu.VMEM),
        scratch_shapes=[
            big, block, big, big, big, big, big,
            big, big, big, block, block, block,
            vectors, vectors, vectors, vectors, vectors, vectors, vectors, pair, pair,
            pltpu.VMEM((3, WALL, EQ, LANES), F32),
            pltpu.VMEM((3, WALL, EQ, LANES), F32),
            pltpu.VMEM((2, SIDE, 8, LANES), F32),
            pltpu.VMEM((2, WALL, 8, LANES), F32),
            pltpu.VMEM((SWEEPS - 1, 2, EQ, LANES), F32),
            pltpu.VMEM((SWEEPS - 1, 2, EQ, LANES), F32),
            pltpu.SemaphoreType.DMA((3, WALL)),
            pltpu.SemaphoreType.DMA((3, WALL)),
            pltpu.SemaphoreType.DMA((2, WALL)),
            pltpu.SemaphoreType.DMA((2, WALL)),
            pltpu.SemaphoreType.DMA((SWEEPS - 1, 2)),
            pltpu.SemaphoreType.DMA((SWEEPS - 1, 2)),
        ],
        compiler_params=pltpu.CompilerParams(collective_id=0, has_side_effects=True),
    )(*arrays)


def solution(mesh):
    return jax.shard_map(
        on_device,
        mesh=mesh,
        in_specs=(
            P("wall", None, "stream"),
            P("wall", None, None, "stream"),
            P("wall", None, None, "stream"),
            P("wall", None, None, "stream"),
            P("wall", None, None, "stream"),
            P("wall", None, None, "stream"),
            P(),
            P("wall", "stream"),
        ),
        out_specs=P("wall", None, "stream"),
        check_vma=False,
    )
```

```python
import jax
import jax.numpy as jnp
from jax import lax
from jax.experimental import pallas as pl
from jax.experimental.pallas import tpu as pltpu
from jax.sharding import PartitionSpec as P

SWEEPS = 3
EQ = 16
CELLS = 8
LANES = 128
WALL = 16
SIDE = 4
BLOCK = EQ * EQ
MESH = pl.DeviceIdType.MESH
F32 = jnp.float32

OFFSETS = sorted(
    [(dy, dx) for dy in range(SIDE) for dx in range(SIDE) if dy or dx],
    key=lambda o: -(min(o[0], SIDE - o[0]) + min(o[1], SIDE - o[1])),
)


def rows(start, size):
    return pl.ds(start, size)


def tree_sum(parts):
    while len(parts) > 1:
        parts = [
            parts[k] + parts[k + 1] if k + 1 < len(parts) else parts[k]
            for k in range(0, len(parts), 2)
        ]
    return parts[0]


def times(blocks, base, vectors, at):
    return tree_sum(
        [
            blocks[rows(base + EQ * k, EQ), :] * vectors[rows(at + k, 1), :]
            for k in range(EQ)
        ]
    )


def block_product(out, out_base, left, left_base, right, right_base, add=None, add_base=0):
    def some_columns(step, carry):
        first = pl.multiple_of(step * (4 * EQ), 4 * EQ)
        sums = [None] * 4
        if add is not None:
            sums = [add[rows(add_base + first + EQ * m, EQ), :] for m in range(4)]
        for k in range(EQ):
            column = left[rows(left_base + EQ * k, EQ), :]
            for m in range(4):
                term = column * right[rows(right_base + first + EQ * m + k, 1), :]
                sums[m] = term if sums[m] is None else sums[m] + term
        for m in range(4):
            out[rows(out_base + first + EQ * m, EQ), :] = sums[m]
        return carry

    lax.fori_loop(0, 4, some_columns, 0)


def swap_four(values, slot, width):
    moved = []
    for u in range(SIDE):
        total = None
        for v in range(SIDE):
            piece = values[v] if u == v else pltpu.roll(values[v], (width * (v - u)) % LANES, 1)
            total = piece if total is None else jnp.where(slot == v, piece, total)
        moved.append(total)
    return moved


def kernel(
    rhs_hbm, pivot_hbm, lower_hbm, upper_hbm, west_hbm, east_hbm, mask_in, codes, out,
    rhs, pivot_in, lower_in, upper_in, west_in, east_in,
    temp, mask_cols, pivot, lower, upper, west, east, c_maps, d_maps, b_maps, others,
    f_rows, q_rows, r_rows, uw_rows, ue_rows, s_rows, ab_rows,
    q_all, r_all, a_all, b_all,
    map_out, map_in, up_out, up_in, back_out, back_in, halo_out, halo_in,
    load_sem, map_send, map_recv, vec_send, vec_recv, halo_send, halo_recv,
):
    me = lax.axis_index("wall")
    stream = lax.axis_index("stream")
    streams = lax.axis_size("stream")
    my_y, my_x = me // SIDE, me % SIDE
    peers = [((my_y + dy) % SIDE) * SIDE + (my_x + dx) % SIDE for dy, dx in OFFSETS]
    next_stream = lax.rem(stream + 1, streams)
    last_stream = lax.rem(stream + streams - 1, streams)
    lane = lax.broadcasted_iota(jnp.int32, (8, LANES), 1)
    lane16 = lax.broadcasted_iota(jnp.int32, (EQ, LANES), 1)
    high_slot, low_slot = lane // 32, (lane // 8) % SIDE

    loads = [
        pltpu.make_async_copy(source, target, load_sem.at[k])
        for k, (source, target) in enumerate(
            [
                (lower_hbm, lower_in),
                (upper_hbm, upper_in),
                (pivot_hbm, pivot_in),
                (rhs_hbm, rhs),
                (west_hbm, west_in),
                (east_hbm, east_in),
            ]
        )
    ]
    for load in loads:
        load.start()

    barrier = pltpu.get_barrier_semaphore()
    for peer in peers:
        pl.semaphore_signal(barrier, inc=1, device_id={"wall": peer}, device_id_type=MESH)
    for other in (next_stream, last_stream):
        pl.semaphore_signal(barrier, inc=1, device_id={"stream": other}, device_id_type=MESH)

    def by_columns(load, source, target, scale=None):
        load.wait()

        def one_cell(j, carry):
            base = pl.multiple_of(j * BLOCK, BLOCK)
            for c in range(EQ):
                temp[rows(base + EQ * c, EQ), :] = source[j, c].astype(F32)
            factor = None if scale is None else scale(j)
            for k in range(EQ):
                column = temp[pl.ds(base + k, EQ, stride=EQ), :]
                if factor is not None:
                    column = column * (mask_cols[EQ * k : EQ * k + EQ, :] * factor)
                target[rows(base + EQ * k, EQ), :] = column
            return carry

        lax.fori_loop(0, CELLS, one_cell, 0)

    def map_copy(which, peer):
        return pltpu.make_async_remote_copy(
            src_ref=map_out.at[which, peer],
            dst_ref=map_in.at[which, me],
            send_sem=map_send.at[which, peer],
            recv_sem=map_recv.at[which, me],
            device_id={"wall": peer},
            device_id_type=MESH,
        )

    def map_arrival(which, peer):
        return pltpu.make_async_remote_copy(
            src_ref=map_out.at[which, peer],
            dst_ref=map_in.at[which, peer],
            send_sem=map_send.at[which, peer],
            recv_sem=map_recv.at[which, peer],
            device_id={"wall": peer},
            device_id_type=MESH,
        )

    def send_map(which, maps, base):
        for half in range(2):
            grid = [
                [maps[rows(base + EQ * (SIDE * high + low) + 8 * half, 8), :] for high in range(SIDE)]
                for low in range(SIDE)
            ]
            grid = [swap_four(values, high_slot, 32) for values in grid]
            for high in range(SIDE):
                values = swap_four([grid[low][high] for low in range(SIDE)], low_slot, 8)
                for low, value in enumerate(values):
                    map_out[which, SIDE * high + low, 8 * half : 8 * half + 8, :] = value
        for peer in peers:
            map_copy(which, peer).start()
        map_in[which, me] = map_out[which, me]

    def take_map(which, carry):
        for peer in peers:
            map_arrival(which, peer).wait_recv()
        for peer in peers:
            map_copy(which, peer).wait_send()
        shifts = [(8 * (my_x - m) + LANES) % LANES for m in range(EQ)]
        for i in range(WALL):
            value = map_in[which, i]
            for m in range(EQ):
                at = pl.multiple_of(which * (WALL * BLOCK) + BLOCK * i + EQ * m, EQ)
                others[rows(at, EQ), :] = pltpu.roll(value, shifts[m], 1)
        return carry

    by_columns(loads[0], lower_in, lower)
    c_maps[0:BLOCK, :] = lower[0:BLOCK, :]

    def c_cell(j, carry):
        base = pl.multiple_of(j * BLOCK, BLOCK)
        block_product(c_maps, base, lower, base, c_maps, base - BLOCK)
        return carry

    lax.fori_loop(1, CELLS, c_cell, 0)
    pl.semaphore_wait(barrier, len(peers) + 2)
    send_map(0, c_maps, (CELLS - 1) * BLOCK)

    by_columns(loads[1], upper_in, upper)
    d_maps[(CELLS - 1) * BLOCK : CELLS * BLOCK, :] = upper[(CELLS - 1) * BLOCK : CELLS * BLOCK, :]
    final = (CELLS - 1) * BLOCK
    b_maps[final : final + BLOCK, :] = c_maps[final : final + BLOCK, :]

    def b_cell(step, carry):
        base = pl.multiple_of((CELLS - 1 - step) * BLOCK, BLOCK)
        block_product(b_maps, base, upper, base, b_maps, base + BLOCK, c_maps, base)
        return carry

    lax.fori_loop(1, CELLS, b_cell, 0)
    send_map(1, b_maps, 0)

    def d_cell(step, carry):
        base = pl.multiple_of((CELLS - 1 - step) * BLOCK, BLOCK)
        block_product(d_maps, base, upper, base, d_maps, base + BLOCK)
        return carry

    lax.fori_loop(1, CELLS, d_cell, 0)
    send_map(2, d_maps, 0)

    def forward_cell(j):
        block = jnp.minimum(j, CELLS - 1)
        base = pl.multiple_of(block * BLOCK, BLOCK)
        at = pl.multiple_of(j * EQ, EQ)
        f_rows[rows(at, EQ), :] = times(pivot, base, s_rows, at)

    def up_cell(j):
        base = pl.multiple_of(j * BLOCK, BLOCK)
        at = pl.multiple_of(j * EQ, EQ)
        q_rows[rows(at, EQ), :] = f_rows[rows(at, EQ), :] + times(lower, base, q_rows, at - EQ)

    def down_chain():
        last = (CELLS - 1) * EQ
        r_rows[last : last + EQ, :] = q_rows[last : last + EQ, :]

        def down(step, carry):
            j = CELLS - 1 - step
            base = pl.multiple_of(j * BLOCK, BLOCK)
            at = pl.multiple_of(j * EQ, EQ)
            r_rows[rows(at, EQ), :] = q_rows[rows(at, EQ), :] + times(upper, base, r_rows, at + EQ)
            return carry

        lax.fori_loop(1, CELLS, down, 0)

    def up_copy(peer):
        return pltpu.make_async_remote_copy(
            src_ref=up_out.at[peer // SIDE],
            dst_ref=up_in.at[me],
            send_sem=vec_send.at[0, peer],
            recv_sem=vec_recv.at[0, me],
            device_id={"wall": peer},
            device_id_type=MESH,
        )

    def up_arrival(peer):
        return pltpu.make_async_remote_copy(
            src_ref=up_out.at[0],
            dst_ref=up_in.at[peer],
            send_sem=vec_send.at[0, peer],
            recv_sem=vec_recv.at[0, peer],
            device_id={"wall": peer},
            device_id_type=MESH,
        )

    def back_copy(peer):
        return pltpu.make_async_remote_copy(
            src_ref=back_out.at[peer],
            dst_ref=back_in.at[me],
            send_sem=vec_send.at[1, peer],
            recv_sem=vec_recv.at[1, me],
            device_id={"wall": peer},
            device_id_type=MESH,
        )

    def back_arrival(peer):
        return pltpu.make_async_remote_copy(
            src_ref=back_out.at[peer],
            dst_ref=back_in.at[peer],
            send_sem=vec_send.at[1, peer],
            recv_sem=vec_recv.at[1, peer],
            device_id={"wall": peer},
            device_id_type=MESH,
        )

    def send_up():
        top = (CELLS - 1) * EQ
        values = [
            q_rows[top : top + 8, :],
            q_rows[top + 8 : top + 16, :],
            r_rows[0:8, :],
            r_rows[8:16, :],
        ]
        for u, value in enumerate(swap_four(values, high_slot, 32)):
            up_out[u] = value
        for peer in peers:
            up_copy(peer).start()
        up_in[me] = up_out[my_y]

    def take_up():
        for peer in peers:
            up_arrival(peer).wait_recv()
        for peer in peers:
            up_copy(peer).wait_send()
        for i in range(WALL):
            tile = up_in[i]
            q_all[EQ * i : EQ * i + 8, :] = tile
            q_all[EQ * i + 8 : EQ * i + 16, :] = pltpu.roll(tile, LANES - 32, 1)
            r_all[EQ * i : EQ * i + 8, :] = pltpu.roll(tile, LANES - 64, 1)
            r_all[EQ * i + 8 : EQ * i + 16, :] = pltpu.roll(tile, LANES - 96, 1)

    def send_back():
        for i in range(WALL):
            tile = a_all[EQ * i : EQ * i + 8, :]
            for v, piece in enumerate(
                [
                    a_all[EQ * i + 8 : EQ * i + 16, :],
                    b_all[EQ * i : EQ * i + 8, :],
                    b_all[EQ * i + 8 : EQ * i + 16, :],
                ]
            ):
                tile = jnp.where(high_slot == v + 1, pltpu.roll(piece, 32 * (v + 1), 1), tile)
            back_out[i] = tile
        for peer in peers:
            back_copy(peer).start()
        back_in[me] = back_out[me]

    def take_back():
        for peer in peers:
            back_arrival(peer).wait_recv()
        for peer in peers:
            back_copy(peer).wait_send()
        values = []
        for high in range(SIDE):
            total = back_in[SIDE * high]
            for low in range(1, SIDE):
                total = jnp.where(low_slot == low, back_in[SIDE * high + low], total)
            values.append(total)
        for v, value in enumerate(swap_four(values, high_slot, 32)):
            ab_rows[8 * v : 8 * v + 8, :] = value

    by_columns(loads[2], pivot_in, pivot)
    loads[3].wait()
    for j in range(CELLS):
        s_rows[EQ * j : EQ * j + EQ, :] = rhs[j]
    forward_cell(0)
    q_rows[0:EQ, :] = f_rows[0:EQ, :]
    forward_cell(1)

    def first_up(j, carry):
        up_cell(j)
        forward_cell(j + 1)
        return carry

    lax.fori_loop(1, CELLS, first_up, 0)
    down_chain()
    send_up()

    for k in range(EQ):
        column = mask_in[:, k : k + 1].astype(F32)
        mask_cols[EQ * k : EQ * k + EQ, :] = jnp.broadcast_to(column, (EQ, LANES))

    def west_on(j):
        code = codes[rows(j, 1), :]
        return jnp.where((code == 0) | (code == 1), 1.0, 0.0).astype(F32)

    def east_on(j):
        code = codes[rows(j, 1), :]
        return jnp.where((code == 0) | (code == 2), 1.0, 0.0).astype(F32)

    by_columns(loads[4], west_in, west, west_on)
    by_columns(loads[5], east_in, east, east_on)
    a_all[0:EQ, :] = jnp.zeros((EQ, LANES), F32)
    b_all[(WALL - 1) * EQ : WALL * EQ, :] = jnp.zeros((EQ, LANES), F32)
    lax.fori_loop(0, 3, take_map, 0)

    def halo_copy(sweep, side, other):
        return pltpu.make_async_remote_copy(
            src_ref=halo_out.at[sweep, side],
            dst_ref=halo_in.at[sweep, side],
            send_sem=halo_send.at[sweep, side],
            recv_sem=halo_recv.at[sweep, side],
            device_id={"stream": other},
            device_id_type=MESH,
        )

    def source_cell(j):
        block = jnp.minimum(j, CELLS - 1)
        base = pl.multiple_of(block * BLOCK, BLOCK)
        at = pl.multiple_of(block * EQ, EQ)
        s_rows[rows(pl.multiple_of(j * EQ, EQ), EQ), :] = (
            rhs[block] - times(west, base, uw_rows, at) - times(east, base, ue_rows, at)
        )

    def one_sweep(sweep, carry):
        take_up()

        a_all[EQ : 2 * EQ, :] = q_all[0:EQ, :]
        maps_b, maps_d = WALL * BLOCK, 2 * WALL * BLOCK

        def rise(i, carry):
            at = pl.multiple_of(i * EQ, EQ)
            base = pl.multiple_of(i * BLOCK, BLOCK)
            a_all[rows(at + EQ, EQ), :] = q_all[rows(at, EQ), :] + times(others, base, a_all, at)
            r_all[rows(at, EQ), :] = r_all[rows(at, EQ), :] + times(others, maps_b + base, a_all, at)
            return carry

        lax.fori_loop(1, WALL - 1, rise, 0)
        last = (WALL - 1) * EQ
        b_all[last - EQ : last, :] = r_all[last : last + EQ, :] + times(
            others, maps_b + (WALL - 1) * BLOCK, a_all, last
        )

        def fall(step, carry):
            i = WALL - 1 - step
            at = pl.multiple_of(i * EQ, EQ)
            base = pl.multiple_of(i * BLOCK, BLOCK)
            b_all[rows(at - EQ, EQ), :] = r_all[rows(at, EQ), :] + times(others, maps_d + base, b_all, at)
            return carry

        lax.fori_loop(1, WALL - 1, fall, 0)
        send_back()
        take_back()

        def update_cell(j, carry):
            base = pl.multiple_of(j * BLOCK, BLOCK)
            at = pl.multiple_of(j * EQ, EQ)
            out[j] = (
                r_rows[rows(at, EQ), :]
                + times(b_maps, base, ab_rows, 0)
                + times(d_maps, base, ab_rows, EQ)
            )
            return carry

        lax.fori_loop(0, CELLS, update_cell, 0)

        @pl.when(sweep < SWEEPS - 1)
        def _():
            to_east = pltpu.roll(out[0], 1, 1)
            to_west = out[0]
            for j in range(1, CELLS):
                to_east = jnp.where(lane16 == j, pltpu.roll(out[j], j + 1, 1), to_east)
                to_west = jnp.where(lane16 == j, pltpu.roll(out[j], j, 1), to_west)
            halo_out[sweep, 0] = to_east
            halo_out[sweep, 1] = to_west
            halo_copy(sweep, 0, next_stream).start()
            halo_copy(sweep, 1, last_stream).start()
            for j in range(CELLS):
                uw_rows[EQ * j : EQ * j + EQ, :] = pltpu.roll(out[j], 1, 1)
                ue_rows[EQ * j : EQ * j + EQ, :] = pltpu.roll(out[j], LANES - 1, 1)
            halo_copy(sweep, 0, next_stream).wait()
            halo_copy(sweep, 1, last_stream).wait()
            from_west = jnp.where(stream == 0, 0.0, halo_in[sweep, 0])
            from_east = jnp.where(stream == streams - 1, 0.0, halo_in[sweep, 1])
            for j in range(CELLS):
                part = slice(EQ * j, EQ * j + EQ)
                ghost = pltpu.roll(from_west, LANES - j, 1) if j else from_west
                uw_rows[part, :] = jnp.where(lane16 == 0, ghost, uw_rows[part, :])
                ghost = pltpu.roll(from_east, LANES - 1 - j, 1)
                ue_rows[part, :] = jnp.where(lane16 == LANES - 1, ghost, ue_rows[part, :])

            source_cell(0)
            source_cell(1)
            forward_cell(0)
            q_rows[0:EQ, :] = f_rows[0:EQ, :]
            source_cell(2)
            forward_cell(1)

            def next_up(j, carry):
                up_cell(j)
                forward_cell(j + 1)
                source_cell(j + 2)
                return carry

            lax.fori_loop(1, CELLS, next_up, 0)
            down_chain()
            send_up()

        return carry

    lax.fori_loop(0, SWEEPS, one_sweep, 0)


def on_device(*arrays):
    big = pltpu.VMEM((CELLS * BLOCK, LANES), F32)
    block = pltpu.VMEM((BLOCK, LANES), F32)
    vectors = pltpu.VMEM((CELLS * EQ, LANES), F32)
    padded = pltpu.VMEM(((CELLS + 2) * EQ, LANES), F32)
    pair = pltpu.VMEM((2 * EQ, LANES), F32)
    wall = pltpu.VMEM((WALL * EQ, LANES), F32)
    narrow = pltpu.VMEM((CELLS, EQ, EQ, LANES), jnp.bfloat16)
    tiles = pltpu.VMEM((WALL, 8, LANES), F32)
    return pl.pallas_call(
        kernel,
        out_shape=jax.ShapeDtypeStruct((CELLS, EQ, LANES), F32),
        in_specs=[pl.BlockSpec(memory_space=pl.ANY)] * 6
        + [pl.BlockSpec(memory_space=pltpu.VMEM)] * 2,
        out_specs=pl.BlockSpec(memory_space=pltpu.VMEM),
        scratch_shapes=[
            pltpu.VMEM((CELLS, EQ, LANES), F32), narrow, narrow, narrow, narrow, narrow,
            big, block, big, big, big, big, big, big, big, big,
            pltpu.VMEM((3 * WALL * BLOCK, LANES), F32),
            padded, vectors, vectors, vectors, vectors, padded, pair,
            wall, wall, wall, wall,
            pltpu.VMEM((3, WALL, EQ, LANES), F32),
            pltpu.VMEM((3, WALL, EQ, LANES), F32),
            pltpu.VMEM((SIDE, 8, LANES), F32), tiles, tiles, tiles,
            pltpu.VMEM((SWEEPS - 1, 2, EQ, LANES), F32),
            pltpu.VMEM((SWEEPS - 1, 2, EQ, LANES), F32),
            pltpu.SemaphoreType.DMA((6,)),
            pltpu.SemaphoreType.DMA((3, WALL)),
            pltpu.SemaphoreType.DMA((3, WALL)),
            pltpu.SemaphoreType.DMA((2, WALL)),
            pltpu.SemaphoreType.DMA((2, WALL)),
            pltpu.SemaphoreType.DMA((SWEEPS - 1, 2)),
            pltpu.SemaphoreType.DMA((SWEEPS - 1, 2)),
        ],
        compiler_params=pltpu.CompilerParams(collective_id=0, has_side_effects=True),
    )(*arrays)


def solution(mesh):
    return jax.shard_map(
        on_device,
        mesh=mesh,
        in_specs=(
            P("wall", None, "stream"),
            P("wall", None, None, "stream"),
            P("wall", None, None, "stream"),
            P("wall", None, None, "stream"),
            P("wall", None, None, "stream"),
            P("wall", None, None, "stream"),
            P(),
            P("wall", "stream"),
        ),
        out_specs=P("wall", None, "stream"),
        check_vma=False,
    )
```

```python
import jax
import jax.numpy as jnp
from jax import lax
from jax.experimental import pallas as pl
from jax.experimental.pallas import tpu as pltpu
from jax.sharding import PartitionSpec as P

SWEEPS = 3
EQ = 16
CELLS = 8
LANES = 128
WALL = 16
SIDE = 4
BLOCK = EQ * EQ
MESH = pl.DeviceIdType.MESH
F32 = jnp.float32

OFFSETS = sorted(
    [(dy, dx) for dy in range(SIDE) for dx in range(SIDE) if dy or dx],
    key=lambda o: -(min(o[0], SIDE - o[0]) + min(o[1], SIDE - o[1])),
)


def rows(start, size):
    return pl.ds(start, size)


def tree_sum(parts):
    while len(parts) > 1:
        parts = [
            parts[k] + parts[k + 1] if k + 1 < len(parts) else parts[k]
            for k in range(0, len(parts), 2)
        ]
    return parts[0]


def times(blocks, base, vectors, at):
    return tree_sum(
        [
            blocks[rows(base + EQ * k, EQ), :] * vectors[rows(at + k, 1), :]
            for k in range(EQ)
        ]
    )


def block_product(out, out_base, left, left_base, right, right_base, add=None, add_base=0):
    for first in range(0, BLOCK, 4 * EQ):
        sums = [None] * 4
        if add is not None:
            sums = [add[rows(add_base + first + EQ * m, EQ), :] for m in range(4)]
        for k in range(EQ):
            column = left[rows(left_base + EQ * k, EQ), :]
            for m in range(4):
                term = column * right[rows(right_base + first + EQ * m + k, 1), :]
                sums[m] = term if sums[m] is None else sums[m] + term
        for m in range(4):
            out[rows(out_base + first + EQ * m, EQ), :] = sums[m]


def swap_four(values, slot, width):
    moved = []
    for u in range(SIDE):
        total = None
        for v in range(SIDE):
            piece = values[v] if u == v else pltpu.roll(values[v], (width * (v - u)) % LANES, 1)
            total = piece if total is None else jnp.where(slot == v, piece, total)
        moved.append(total)
    return moved


def kernel(
    rhs_hbm, pivot_hbm, lower_hbm, upper_hbm, west_hbm, east_hbm, mask_hbm, codes_hbm, out,
    rhs, pivot_in, lower_in, upper_in, west_in, east_in, mask_in, codes,
    temp, mask_cols, pivot, lower, upper, west, east, c_maps, d_maps, b_maps, others,
    f_rows, q_rows, r_rows, uw_rows, ue_rows, s_rows, ab_rows,
    q_all, r_all, a_all, b_all,
    map_out, map_in, up_out, up_in, back_out, back_in, halo_out, halo_in,
    load_sem, map_send, map_recv, vec_send, vec_recv, halo_send, halo_recv,
):
    me = lax.axis_index("wall")
    stream = lax.axis_index("stream")
    streams = lax.axis_size("stream")
    my_y, my_x = me // SIDE, me % SIDE
    peers = [((my_y + dy) % SIDE) * SIDE + (my_x + dx) % SIDE for dy, dx in OFFSETS]
    next_stream = lax.rem(stream + 1, streams)
    last_stream = lax.rem(stream + streams - 1, streams)
    lane = lax.broadcasted_iota(jnp.int32, (8, LANES), 1)
    lane16 = lax.broadcasted_iota(jnp.int32, (EQ, LANES), 1)
    high_slot, low_slot = lane // 32, (lane // 8) % SIDE

    loads = [
        pltpu.make_async_copy(source, target, load_sem.at[k])
        for k, (source, target) in enumerate(
            [
                (lower_hbm, lower_in),
                (upper_hbm, upper_in),
                (pivot_hbm, pivot_in),
                (rhs_hbm, rhs),
                (west_hbm, west_in),
                (east_hbm, east_in),
                (mask_hbm, mask_in),
                (codes_hbm, codes),
            ]
        )
    ]
    for load in loads:
        load.start()

    barrier = pltpu.get_barrier_semaphore()
    for peer in peers:
        pl.semaphore_signal(barrier, inc=1, device_id={"wall": peer}, device_id_type=MESH)
    for other in (next_stream, last_stream):
        pl.semaphore_signal(barrier, inc=1, device_id={"stream": other}, device_id_type=MESH)

    def column_cell(j, source, target, scale=None):
        base = pl.multiple_of(j * BLOCK, BLOCK)
        for c in range(EQ):
            temp[rows(base + EQ * c, EQ), :] = source[j, c].astype(F32)
        factor = None if scale is None else scale(j)
        for k in range(EQ):
            column = temp[pl.ds(base + k, EQ, stride=EQ), :]
            if factor is not None:
                column = column * (mask_cols[EQ * k : EQ * k + EQ, :] * factor)
            target[rows(base + EQ * k, EQ), :] = column

    def by_columns(source, target, scale=None):
        def one_cell(j, carry):
            column_cell(j, source, target, scale)
            return carry

        lax.fori_loop(0, CELLS, one_cell, 0)

    def map_copy(which, peer):
        return pltpu.make_async_remote_copy(
            src_ref=map_out.at[which, peer],
            dst_ref=map_in.at[which, me],
            send_sem=map_send.at[which, peer],
            recv_sem=map_recv.at[which, me],
            device_id={"wall": peer},
            device_id_type=MESH,
        )

    def map_arrival(which, peer):
        return pltpu.make_async_remote_copy(
            src_ref=map_out.at[which, peer],
            dst_ref=map_in.at[which, peer],
            send_sem=map_send.at[which, peer],
            recv_sem=map_recv.at[which, peer],
            device_id={"wall": peer},
            device_id_type=MESH,
        )

    def send_map(which, maps, base):
        for half in range(2):
            grid = [
                [maps[rows(base + EQ * (SIDE * high + low) + 8 * half, 8), :] for high in range(SIDE)]
                for low in range(SIDE)
            ]
            grid = [swap_four(values, high_slot, 32) for values in grid]
            for high in range(SIDE):
                values = swap_four([grid[low][high] for low in range(SIDE)], low_slot, 8)
                for low, value in enumerate(values):
                    map_out[which, SIDE * high + low, 8 * half : 8 * half + 8, :] = value
        for peer in peers:
            map_copy(which, peer).start()
        map_in[which, me] = map_out[which, me]

    def take_map(which, carry):
        for peer in peers:
            map_arrival(which, peer).wait_recv()
        for peer in peers:
            map_copy(which, peer).wait_send()
        shifts = [(8 * (my_x - m) + LANES) % LANES for m in range(EQ)]
        for i in range(WALL):
            value = map_in[which, i]
            for m in range(EQ):
                at = pl.multiple_of(which * (WALL * BLOCK) + BLOCK * i + EQ * m, EQ)
                others[rows(at, EQ), :] = pltpu.roll(value, shifts[m], 1)
        return carry

    loads[0].wait()
    by_columns(lower_in, lower)
    loads[1].wait()
    column_cell(0, upper_in, upper)
    c_maps[0:BLOCK, :] = lower[0:BLOCK, :]

    def c_cell(j, carry):
        base = pl.multiple_of(j * BLOCK, BLOCK)
        block_product(c_maps, base, lower, base, c_maps, base - BLOCK)
        column_cell(j, upper_in, upper)
        return carry

    lax.fori_loop(1, CELLS, c_cell, 0)
    pl.semaphore_wait(barrier, len(peers) + 2)
    send_map(0, c_maps, (CELLS - 1) * BLOCK)

    loads[2].wait()
    column_cell(0, pivot_in, pivot)
    d_maps[(CELLS - 1) * BLOCK : CELLS * BLOCK, :] = upper[(CELLS - 1) * BLOCK : CELLS * BLOCK, :]
    final = (CELLS - 1) * BLOCK
    b_maps[final : final + BLOCK, :] = c_maps[final : final + BLOCK, :]

    def b_cell(step, carry):
        base = pl.multiple_of((CELLS - 1 - step) * BLOCK, BLOCK)
        block_product(b_maps, base, upper, base, b_maps, base + BLOCK, c_maps, base)
        column_cell(step, pivot_in, pivot)
        return carry

    lax.fori_loop(1, CELLS, b_cell, 0)
    send_map(1, b_maps, 0)

    def forward_cell(j):
        block = jnp.minimum(j, CELLS - 1)
        base = pl.multiple_of(block * BLOCK, BLOCK)
        at = pl.multiple_of(j * EQ, EQ)
        f_rows[rows(at, EQ), :] = times(pivot, base, s_rows, at)

    def up_cell(j):
        base = pl.multiple_of(j * BLOCK, BLOCK)
        at = pl.multiple_of(j * EQ, EQ)
        q_rows[rows(at, EQ), :] = f_rows[rows(at, EQ), :] + times(lower, base, q_rows, at - EQ)

    def down_chain():
        last = (CELLS - 1) * EQ
        r_rows[last : last + EQ, :] = q_rows[last : last + EQ, :]

        def down(step, carry):
            j = CELLS - 1 - step
            base = pl.multiple_of(j * BLOCK, BLOCK)
            at = pl.multiple_of(j * EQ, EQ)
            r_rows[rows(at, EQ), :] = q_rows[rows(at, EQ), :] + times(upper, base, r_rows, at + EQ)
            return carry

        lax.fori_loop(1, CELLS, down, 0)

    def up_copy(peer):
        return pltpu.make_async_remote_copy(
            src_ref=up_out.at[peer // SIDE],
            dst_ref=up_in.at[me],
            send_sem=vec_send.at[0, peer],
            recv_sem=vec_recv.at[0, me],
            device_id={"wall": peer},
            device_id_type=MESH,
        )

    def up_arrival(peer):
        return pltpu.make_async_remote_copy(
            src_ref=up_out.at[0],
            dst_ref=up_in.at[peer],
            send_sem=vec_send.at[0, peer],
            recv_sem=vec_recv.at[0, peer],
            device_id={"wall": peer},
            device_id_type=MESH,
        )

    def back_copy(peer):
        return pltpu.make_async_remote_copy(
            src_ref=back_out.at[peer],
            dst_ref=back_in.at[me],
            send_sem=vec_send.at[1, peer],
            recv_sem=vec_recv.at[1, me],
            device_id={"wall": peer},
            device_id_type=MESH,
        )

    def back_arrival(peer):
        return pltpu.make_async_remote_copy(
            src_ref=back_out.at[peer],
            dst_ref=back_in.at[peer],
            send_sem=vec_send.at[1, peer],
            recv_sem=vec_recv.at[1, peer],
            device_id={"wall": peer},
            device_id_type=MESH,
        )

    def send_up():
        top = (CELLS - 1) * EQ
        values = [
            q_rows[top : top + 8, :],
            q_rows[top + 8 : top + 16, :],
            r_rows[0:8, :],
            r_rows[8:16, :],
        ]
        for u, value in enumerate(swap_four(values, high_slot, 32)):
            up_out[u] = value
        for peer in peers:
            up_copy(peer).start()
        up_in[me] = up_out[my_y]

    def take_up():
        for peer in peers:
            up_arrival(peer).wait_recv()
        for peer in peers:
            up_copy(peer).wait_send()
        for i in range(WALL):
            tile = up_in[i]
            q_all[EQ * i : EQ * i + 8, :] = tile
            q_all[EQ * i + 8 : EQ * i + 16, :] = pltpu.roll(tile, LANES - 32, 1)
            r_all[EQ * i : EQ * i + 8, :] = pltpu.roll(tile, LANES - 64, 1)
            r_all[EQ * i + 8 : EQ * i + 16, :] = pltpu.roll(tile, LANES - 96, 1)

    def send_back():
        for i in range(WALL):
            tile = a_all[EQ * i : EQ * i + 8, :]
            for v, piece in enumerate(
                [
                    a_all[EQ * i + 8 : EQ * i + 16, :],
                    b_all[EQ * i : EQ * i + 8, :],
                    b_all[EQ * i + 8 : EQ * i + 16, :],
                ]
            ):
                tile = jnp.where(high_slot == v + 1, pltpu.roll(piece, 32 * (v + 1), 1), tile)
            back_out[i] = tile
        for peer in peers:
            back_copy(peer).start()
        back_in[me] = back_out[me]

    def take_back():
        for peer in peers:
            back_arrival(peer).wait_recv()
        for peer in peers:
            back_copy(peer).wait_send()
        values = []
        for high in range(SIDE):
            total = back_in[SIDE * high]
            for low in range(1, SIDE):
                total = jnp.where(low_slot == low, back_in[SIDE * high + low], total)
            values.append(total)
        for v, value in enumerate(swap_four(values, high_slot, 32)):
            ab_rows[8 * v : 8 * v + 8, :] = value

    loads[3].wait()
    for j in range(CELLS):
        s_rows[EQ * j : EQ * j + EQ, :] = rhs[j]
    forward_cell(0)
    q_rows[0:EQ, :] = f_rows[0:EQ, :]
    forward_cell(1)

    def first_up(j, carry):
        up_cell(j)
        forward_cell(j + 1)
        return carry

    lax.fori_loop(1, CELLS, first_up, 0)
    down_chain()
    send_up()

    def d_cell(step, carry):
        base = pl.multiple_of((CELLS - 1 - step) * BLOCK, BLOCK)
        block_product(d_maps, base, upper, base, d_maps, base + BLOCK)
        return carry

    lax.fori_loop(1, CELLS, d_cell, 0)
    send_map(2, d_maps, 0)

    loads[6].wait()
    loads[7].wait()

    for k in range(EQ):
        column = mask_in[:, k : k + 1].astype(F32)
        mask_cols[EQ * k : EQ * k + EQ, :] = jnp.broadcast_to(column, (EQ, LANES))

    def west_on(j):
        code = codes[rows(j, 1), :]
        return jnp.where((code == 0) | (code == 1), 1.0, 0.0).astype(F32)

    def east_on(j):
        code = codes[rows(j, 1), :]
        return jnp.where((code == 0) | (code == 2), 1.0, 0.0).astype(F32)

    loads[4].wait()
    by_columns(west_in, west, west_on)
    loads[5].wait()
    by_columns(east_in, east, east_on)
    a_all[0:EQ, :] = jnp.zeros((EQ, LANES), F32)
    b_all[(WALL - 1) * EQ : WALL * EQ, :] = jnp.zeros((EQ, LANES), F32)

    def halo_copy(sweep, side, other):
        return pltpu.make_async_remote_copy(
            src_ref=halo_out.at[sweep, side],
            dst_ref=halo_in.at[sweep, side],
            send_sem=halo_send.at[sweep, side],
            recv_sem=halo_recv.at[sweep, side],
            device_id={"stream": other},
            device_id_type=MESH,
        )

    def source_cell(j):
        block = jnp.minimum(j, CELLS - 1)
        base = pl.multiple_of(block * BLOCK, BLOCK)
        at = pl.multiple_of(block * EQ, EQ)
        s_rows[rows(pl.multiple_of(j * EQ, EQ), EQ), :] = (
            rhs[block] - times(west, base, uw_rows, at) - times(east, base, ue_rows, at)
        )

    maps_b, maps_d = WALL * BLOCK, 2 * WALL * BLOCK

    def rise():
        a_all[EQ : 2 * EQ, :] = q_all[0:EQ, :]
        for i in range(1, WALL):
            part = slice(EQ * i, EQ * i + EQ)
            if i < WALL - 1:
                a_all[EQ * i + EQ : EQ * i + 2 * EQ, :] = q_all[part, :] + times(
                    others, BLOCK * i, a_all, EQ * i
                )
            total = r_all[part, :] + times(others, maps_b + BLOCK * i, a_all, EQ * i)
            if i < WALL - 1:
                r_all[part, :] = total
            else:
                b_all[EQ * i - EQ : EQ * i, :] = total

    lax.fori_loop(0, 2, take_map, 0)
    take_up()
    rise()
    take_map(2, 0)

    def one_sweep(sweep, carry):
        for step in range(1, WALL - 1):
            i = WALL - 1 - step
            b_all[EQ * i - EQ : EQ * i, :] = r_all[EQ * i : EQ * i + EQ, :] + times(
                others, maps_d + BLOCK * i, b_all, EQ * i
            )
        send_back()
        take_back()

        def update_cell(j, carry):
            base = pl.multiple_of(j * BLOCK, BLOCK)
            at = pl.multiple_of(j * EQ, EQ)
            out[j] = (
                r_rows[rows(at, EQ), :]
                + times(b_maps, base, ab_rows, 0)
                + times(d_maps, base, ab_rows, EQ)
            )
            return carry

        lax.fori_loop(0, CELLS, update_cell, 0)

        @pl.when(sweep < SWEEPS - 1)
        def _():
            to_east = pltpu.roll(out[0], 1, 1)
            to_west = out[0]
            for j in range(1, CELLS):
                to_east = jnp.where(lane16 == j, pltpu.roll(out[j], j + 1, 1), to_east)
                to_west = jnp.where(lane16 == j, pltpu.roll(out[j], j, 1), to_west)
            halo_out[sweep, 0] = to_east
            halo_out[sweep, 1] = to_west
            halo_copy(sweep, 0, next_stream).start()
            halo_copy(sweep, 1, last_stream).start()
            for j in range(CELLS):
                uw_rows[EQ * j : EQ * j + EQ, :] = pltpu.roll(out[j], 1, 1)
                ue_rows[EQ * j : EQ * j + EQ, :] = pltpu.roll(out[j], LANES - 1, 1)
            halo_copy(sweep, 0, next_stream).wait()
            halo_copy(sweep, 1, last_stream).wait()
            from_west = jnp.where(stream == 0, 0.0, halo_in[sweep, 0])
            from_east = jnp.where(stream == streams - 1, 0.0, halo_in[sweep, 1])
            for j in range(CELLS):
                part = slice(EQ * j, EQ * j + EQ)
                ghost = pltpu.roll(from_west, LANES - j, 1) if j else from_west
                uw_rows[part, :] = jnp.where(lane16 == 0, ghost, uw_rows[part, :])
                ghost = pltpu.roll(from_east, LANES - 1 - j, 1)
                ue_rows[part, :] = jnp.where(lane16 == LANES - 1, ghost, ue_rows[part, :])

            source_cell(0)
            source_cell(1)
            forward_cell(0)
            q_rows[0:EQ, :] = f_rows[0:EQ, :]
            source_cell(2)
            forward_cell(1)

            def next_up(j, carry):
                up_cell(j)
                forward_cell(j + 1)
                source_cell(j + 2)
                return carry

            lax.fori_loop(1, CELLS, next_up, 0)
            down_chain()
            send_up()
            take_up()
            rise()

        return carry

    lax.fori_loop(0, SWEEPS, one_sweep, 0)


def on_device(*arrays):
    big = pltpu.VMEM((CELLS * BLOCK, LANES), F32)
    block = pltpu.VMEM((BLOCK, LANES), F32)
    vectors = pltpu.VMEM((CELLS * EQ, LANES), F32)
    padded = pltpu.VMEM(((CELLS + 2) * EQ, LANES), F32)
    pair = pltpu.VMEM((2 * EQ, LANES), F32)
    wall = pltpu.VMEM((WALL * EQ, LANES), F32)
    narrow = pltpu.VMEM((CELLS, EQ, EQ, LANES), jnp.bfloat16)
    tiles = pltpu.VMEM((WALL, 8, LANES), F32)
    return pl.pallas_call(
        kernel,
        out_shape=jax.ShapeDtypeStruct((CELLS, EQ, LANES), F32),
        in_specs=[pl.BlockSpec(memory_space=pltpu.HBM)] * 8,
        out_specs=pl.BlockSpec(memory_space=pltpu.VMEM),
        scratch_shapes=[
            pltpu.VMEM((CELLS, EQ, LANES), F32), narrow, narrow, narrow, narrow, narrow,
            pltpu.VMEM((EQ, EQ), jnp.int32), pltpu.VMEM((CELLS, LANES), jnp.int32),
            big, block, big, big, big, big, big, big, big, big,
            pltpu.VMEM((3 * WALL * BLOCK, LANES), F32),
            padded, vectors, vectors, vectors, vectors, padded, pair,
            wall, wall, wall, wall,
            pltpu.VMEM((3, WALL, EQ, LANES), F32),
            pltpu.VMEM((3, WALL, EQ, LANES), F32),
            pltpu.VMEM((SIDE, 8, LANES), F32), tiles, tiles, tiles,
            pltpu.VMEM((SWEEPS - 1, 2, EQ, LANES), F32),
            pltpu.VMEM((SWEEPS - 1, 2, EQ, LANES), F32),
            pltpu.SemaphoreType.DMA((8,)),
            pltpu.SemaphoreType.DMA((3, WALL)),
            pltpu.SemaphoreType.DMA((3, WALL)),
            pltpu.SemaphoreType.DMA((2, WALL)),
            pltpu.SemaphoreType.DMA((2, WALL)),
            pltpu.SemaphoreType.DMA((SWEEPS - 1, 2)),
            pltpu.SemaphoreType.DMA((SWEEPS - 1, 2)),
        ],
        compiler_params=pltpu.CompilerParams(collective_id=0, has_side_effects=True),
    )(*arrays)


def solution(mesh):
    return jax.shard_map(
        on_device,
        mesh=mesh,
        in_specs=(
            P("wall", None, "stream"),
            P("wall", None, None, "stream"),
            P("wall", None, None, "stream"),
            P("wall", None, None, "stream"),
            P("wall", None, None, "stream"),
            P("wall", None, None, "stream"),
            P(),
            P("wall", "stream"),
        ),
        out_specs=P("wall", None, "stream"),
        check_vma=False,
    )
```

```python
import jax
import jax.numpy as jnp
from jax import lax
from jax.experimental import pallas as pl
from jax.experimental.pallas import tpu as pltpu
from jax.sharding import PartitionSpec as P

SWEEPS = 3
EQ = 16
CELLS = 8
LANES = 128
WALL = 16
SIDE = 4
BLOCK = EQ * EQ
MESH = pl.DeviceIdType.MESH
F32 = jnp.float32

OFFSETS = sorted(
    [(dy, dx) for dy in range(SIDE) for dx in range(SIDE) if dy or dx],
    key=lambda o: -(min(o[0], SIDE - o[0]) + min(o[1], SIDE - o[1])),
)


def rows(start, size):
    return pl.ds(start, size)


def tree_sum(parts):
    while len(parts) > 1:
        parts = [
            parts[k] + parts[k + 1] if k + 1 < len(parts) else parts[k]
            for k in range(0, len(parts), 2)
        ]
    return parts[0]


def times(blocks, base, vectors, at):
    return tree_sum(
        [
            blocks[rows(base + EQ * k, EQ), :] * vectors[rows(at + k, 1), :]
            for k in range(EQ)
        ]
    )


def block_product(out, out_base, left, left_base, right, right_base, add=None, add_base=0):
    for first in range(0, BLOCK, 4 * EQ):
        sums = [None] * 4
        if add is not None:
            sums = [add[rows(add_base + first + EQ * m, EQ), :] for m in range(4)]
        for k in range(EQ):
            column = left[rows(left_base + EQ * k, EQ), :]
            for m in range(4):
                term = column * right[rows(right_base + first + EQ * m + k, 1), :]
                sums[m] = term if sums[m] is None else sums[m] + term
        for m in range(4):
            out[rows(out_base + first + EQ * m, EQ), :] = sums[m]


def swap_four(values, slot, width):
    moved = []
    for u in range(SIDE):
        total = None
        for v in range(SIDE):
            piece = values[v] if u == v else pltpu.roll(values[v], (width * (v - u)) % LANES, 1)
            total = piece if total is None else jnp.where(slot == v, piece, total)
        moved.append(total)
    return moved


def kernel(
    rhs_hbm, pivot_hbm, lower_hbm, upper_hbm, west_hbm, east_hbm, mask_hbm, codes_hbm, out,
    rhs, pivot_in, lower_in, upper_in, west_in, east_in, mask_in, codes,
    temp, mask_cols, pivot, lower, upper, west, east, c_maps, d_maps, b_maps, others,
    f_rows, q_rows, r_rows, uw_rows, ue_rows, s_rows, ab_rows,
    q_all, r_all, a_all, b_all,
    map_out, map_in, up_out, up_in, back_out, back_in, halo_out, halo_in,
    edge_out, edge_in, b_edge, d_edge, ghost_in, ghost_ab,
    load_sem, map_send, map_recv, vec_send, vec_recv, halo_send, halo_recv,
    edge_send, edge_recv, ghost_send, ghost_recv, ready,
):
    me = lax.axis_index("wall")
    stream = lax.axis_index("stream")
    streams = lax.axis_size("stream")
    my_y, my_x = me // SIDE, me % SIDE
    peers = [((my_y + dy) % SIDE) * SIDE + (my_x + dx) % SIDE for dy, dx in OFFSETS]
    next_stream = lax.rem(stream + 1, streams)
    last_stream = lax.rem(stream + streams - 1, streams)
    lane = lax.broadcasted_iota(jnp.int32, (8, LANES), 1)
    lane16 = lax.broadcasted_iota(jnp.int32, (EQ, LANES), 1)
    high_slot, low_slot = lane // 32, (lane // 8) % SIDE

    loads = [
        pltpu.make_async_copy(source, target, load_sem.at[k])
        for k, (source, target) in enumerate(
            [
                (lower_hbm, lower_in),
                (upper_hbm, upper_in),
                (pivot_hbm, pivot_in),
                (rhs_hbm, rhs),
                (west_hbm, west_in),
                (east_hbm, east_in),
                (mask_hbm, mask_in),
                (codes_hbm, codes),
            ]
        )
    ]
    for load in loads:
        load.start()

    barrier = pltpu.get_barrier_semaphore()
    for peer in peers:
        pl.semaphore_signal(barrier, inc=1, device_id={"wall": peer}, device_id_type=MESH)
    for other in (next_stream, last_stream):
        pl.semaphore_signal(barrier, inc=1, device_id={"stream": other}, device_id_type=MESH)

    def column_cell(j, source, target, scale=None):
        base = pl.multiple_of(j * BLOCK, BLOCK)
        for c in range(EQ):
            temp[rows(base + EQ * c, EQ), :] = source[j, c].astype(F32)
        factor = None if scale is None else scale(j)
        for k in range(EQ):
            column = temp[pl.ds(base + k, EQ, stride=EQ), :]
            if factor is not None:
                column = column * (mask_cols[EQ * k : EQ * k + EQ, :] * factor)
            target[rows(base + EQ * k, EQ), :] = column

    def by_columns(source, target, scale=None):
        def one_cell(j, carry):
            column_cell(j, source, target, scale)
            return carry

        lax.fori_loop(0, CELLS, one_cell, 0)

    def map_copy(which, peer):
        return pltpu.make_async_remote_copy(
            src_ref=map_out.at[which, peer],
            dst_ref=map_in.at[which, me],
            send_sem=map_send.at[which, peer],
            recv_sem=map_recv.at[which, me],
            device_id={"wall": peer},
            device_id_type=MESH,
        )

    def map_arrival(which, peer):
        return pltpu.make_async_remote_copy(
            src_ref=map_out.at[which, peer],
            dst_ref=map_in.at[which, peer],
            send_sem=map_send.at[which, peer],
            recv_sem=map_recv.at[which, peer],
            device_id={"wall": peer},
            device_id_type=MESH,
        )

    def send_map(which, maps, base):
        for half in range(2):
            grid = [
                [maps[rows(base + EQ * (SIDE * high + low) + 8 * half, 8), :] for high in range(SIDE)]
                for low in range(SIDE)
            ]
            grid = [swap_four(values, high_slot, 32) for values in grid]
            for high in range(SIDE):
                values = swap_four([grid[low][high] for low in range(SIDE)], low_slot, 8)
                for low, value in enumerate(values):
                    map_out[which, SIDE * high + low, 8 * half : 8 * half + 8, :] = value
        for peer in peers:
            map_copy(which, peer).start()
        map_in[which, me] = map_out[which, me]

    def take_map(which, carry):
        for peer in peers:
            map_arrival(which, peer).wait_recv()
        for peer in peers:
            map_copy(which, peer).wait_send()
        shifts = [(8 * (my_x - m) + LANES) % LANES for m in range(EQ)]
        for i in range(WALL):
            value = map_in[which, i]
            for m in range(EQ):
                at = pl.multiple_of(which * (WALL * BLOCK) + BLOCK * i + EQ * m, EQ)
                others[rows(at, EQ), :] = pltpu.roll(value, shifts[m], 1)
        return carry

    loads[0].wait()
    by_columns(lower_in, lower)
    loads[1].wait()
    column_cell(0, upper_in, upper)
    c_maps[0:BLOCK, :] = lower[0:BLOCK, :]

    def c_cell(j, carry):
        base = pl.multiple_of(j * BLOCK, BLOCK)
        block_product(c_maps, base, lower, base, c_maps, base - BLOCK)
        column_cell(j, upper_in, upper)
        return carry

    lax.fori_loop(1, CELLS, c_cell, 0)
    pl.semaphore_wait(barrier, len(peers) + 2)

    for owner in (WALL - 1, 0):

        @pl.when(me != owner)
        def _():
            pl.semaphore_signal(ready, inc=1, device_id={"wall": owner}, device_id_type=MESH)

    send_map(0, c_maps, (CELLS - 1) * BLOCK)

    loads[2].wait()
    column_cell(0, pivot_in, pivot)
    d_maps[(CELLS - 1) * BLOCK : CELLS * BLOCK, :] = upper[(CELLS - 1) * BLOCK : CELLS * BLOCK, :]
    final = (CELLS - 1) * BLOCK
    b_maps[final : final + BLOCK, :] = c_maps[final : final + BLOCK, :]

    def b_cell(step, carry):
        base = pl.multiple_of((CELLS - 1 - step) * BLOCK, BLOCK)
        block_product(b_maps, base, upper, base, b_maps, base + BLOCK, c_maps, base)
        column_cell(step, pivot_in, pivot)
        return carry

    lax.fori_loop(1, CELLS, b_cell, 0)
    send_map(1, b_maps, 0)

    def forward_cell(j):
        block = jnp.minimum(j, CELLS - 1)
        base = pl.multiple_of(block * BLOCK, BLOCK)
        at = pl.multiple_of(j * EQ, EQ)
        f_rows[rows(at, EQ), :] = times(pivot, base, s_rows, at)

    def up_cell(j):
        base = pl.multiple_of(j * BLOCK, BLOCK)
        at = pl.multiple_of(j * EQ, EQ)
        q_rows[rows(at, EQ), :] = f_rows[rows(at, EQ), :] + times(lower, base, q_rows, at - EQ)

    def down_chain():
        last = (CELLS - 1) * EQ
        r_rows[last : last + EQ, :] = q_rows[last : last + EQ, :]

        def down(step, carry):
            j = CELLS - 1 - step
            base = pl.multiple_of(j * BLOCK, BLOCK)
            at = pl.multiple_of(j * EQ, EQ)
            r_rows[rows(at, EQ), :] = q_rows[rows(at, EQ), :] + times(upper, base, r_rows, at + EQ)
            return carry

        lax.fori_loop(1, CELLS, down, 0)

    def up_copy(peer):
        return pltpu.make_async_remote_copy(
            src_ref=up_out.at[peer // SIDE],
            dst_ref=up_in.at[me],
            send_sem=vec_send.at[0, peer],
            recv_sem=vec_recv.at[0, me],
            device_id={"wall": peer},
            device_id_type=MESH,
        )

    def up_arrival(peer):
        return pltpu.make_async_remote_copy(
            src_ref=up_out.at[0],
            dst_ref=up_in.at[peer],
            send_sem=vec_send.at[0, peer],
            recv_sem=vec_recv.at[0, peer],
            device_id={"wall": peer},
            device_id_type=MESH,
        )

    def back_copy(peer):
        return pltpu.make_async_remote_copy(
            src_ref=back_out.at[peer],
            dst_ref=back_in.at[me],
            send_sem=vec_send.at[1, peer],
            recv_sem=vec_recv.at[1, me],
            device_id={"wall": peer},
            device_id_type=MESH,
        )

    def back_arrival(peer):
        return pltpu.make_async_remote_copy(
            src_ref=back_out.at[peer],
            dst_ref=back_in.at[peer],
            send_sem=vec_send.at[1, peer],
            recv_sem=vec_recv.at[1, peer],
            device_id={"wall": peer},
            device_id_type=MESH,
        )

    def send_up():
        top = (CELLS - 1) * EQ
        values = [
            q_rows[top : top + 8, :],
            q_rows[top + 8 : top + 16, :],
            r_rows[0:8, :],
            r_rows[8:16, :],
        ]
        for u, value in enumerate(swap_four(values, high_slot, 32)):
            up_out[u] = value
        for peer in peers:
            up_copy(peer).start()
        up_in[me] = up_out[my_y]

    def take_up():
        for peer in peers:
            up_arrival(peer).wait_recv()
        for peer in peers:
            up_copy(peer).wait_send()
        for i in range(WALL):
            tile = up_in[i]
            q_all[EQ * i : EQ * i + 8, :] = tile
            q_all[EQ * i + 8 : EQ * i + 16, :] = pltpu.roll(tile, LANES - 32, 1)
            r_all[EQ * i : EQ * i + 8, :] = pltpu.roll(tile, LANES - 64, 1)
            r_all[EQ * i + 8 : EQ * i + 16, :] = pltpu.roll(tile, LANES - 96, 1)

    def ghost_copy(sweep, side, i):
        return pltpu.make_async_remote_copy(
            src_ref=back_out.at[i],
            dst_ref=ghost_in.at[sweep, side],
            send_sem=ghost_send.at[sweep, i],
            recv_sem=ghost_recv.at[sweep, side],
            device_id={"wall": i, "stream": last_stream if side else next_stream},
            device_id_type=MESH,
        )

    def on_ghosts(sweep, act):
        for side, owner in ((0, WALL - 1), (1, 0)):

            @pl.when((sweep < SWEEPS - 1) & (me == owner))
            def _():
                for i in range(WALL):
                    act(ghost_copy(sweep, side, i))

    def pack_edges(values):
        to_next, to_last = None, None
        for j, value in enumerate(values):
            high, low = pltpu.roll(value, j + 1, 1), pltpu.roll(value, 8 + j, 1)
            to_next = high if j == 0 else jnp.where(lane16 == j, high, to_next)
            to_last = low if j == 0 else jnp.where(lane16 == 8 + j, low, to_last)
        return to_next, to_last

    def edge_copy(side, other):
        return pltpu.make_async_remote_copy(
            src_ref=edge_out.at[side],
            dst_ref=edge_in.at[side],
            send_sem=edge_send.at[side],
            recv_sem=edge_recv.at[side],
            device_id={"stream": other},
            device_id_type=MESH,
        )

    def send_edge_maps():
        def some_columns(step, carry):
            for m in range(8):
                at = pl.multiple_of(step * (8 * EQ) + EQ * m, EQ)
                for which, maps in enumerate((b_maps, d_maps)):
                    pair = pack_edges([maps[rows(BLOCK * j + at, EQ), :] for j in range(CELLS)])
                    for side in range(2):
                        edge_out[side, which, rows(at, EQ), :] = pair[side]
            return carry

        lax.fori_loop(0, 2, some_columns, 0)
        edge_copy(0, next_stream).start()
        edge_copy(1, last_stream).start()

    def take_edge_maps():
        edge_copy(0, next_stream).wait()
        edge_copy(1, last_stream).wait()
        for m in range(EQ):
            part = slice(EQ * m, EQ * m + EQ)
            for which, maps in enumerate((b_edge, d_edge)):
                maps[part, :] = jnp.where(
                    lane16 < 8, edge_in[0, which, part, :], edge_in[1, which, part, :]
                )

    def send_back(sweep):
        for i in range(WALL):
            tile = a_all[EQ * i : EQ * i + 8, :]
            for v, piece in enumerate(
                [
                    a_all[EQ * i + 8 : EQ * i + 16, :],
                    b_all[EQ * i : EQ * i + 8, :],
                    b_all[EQ * i + 8 : EQ * i + 16, :],
                ]
            ):
                tile = jnp.where(high_slot == v + 1, pltpu.roll(piece, 32 * (v + 1), 1), tile)
            back_out[i] = tile

        @pl.when((sweep == 0) & (me % (WALL - 1) == 0))
        def _():
            pl.semaphore_wait(ready, WALL - 1)

        on_ghosts(sweep, lambda copy: copy.start())
        for peer in peers:
            back_copy(peer).start()
        back_in[me] = back_out[me]

    def take_back():
        for peer in peers:
            back_arrival(peer).wait_recv()
        for peer in peers:
            back_copy(peer).wait_send()
        values = []
        for high in range(SIDE):
            total = back_in[SIDE * high]
            for low in range(1, SIDE):
                total = jnp.where(low_slot == low, back_in[SIDE * high + low], total)
            values.append(total)
        for v, value in enumerate(swap_four(values, high_slot, 32)):
            ab_rows[8 * v : 8 * v + 8, :] = value

    loads[3].wait()
    for j in range(CELLS):
        s_rows[EQ * j : EQ * j + EQ, :] = rhs[j]
    forward_cell(0)
    q_rows[0:EQ, :] = f_rows[0:EQ, :]
    forward_cell(1)

    def first_up(j, carry):
        up_cell(j)
        forward_cell(j + 1)
        return carry

    lax.fori_loop(1, CELLS, first_up, 0)
    down_chain()
    send_up()

    def d_cell(step, carry):
        base = pl.multiple_of((CELLS - 1 - step) * BLOCK, BLOCK)
        block_product(d_maps, base, upper, base, d_maps, base + BLOCK)
        return carry

    lax.fori_loop(1, CELLS, d_cell, 0)
    send_map(2, d_maps, 0)

    loads[6].wait()
    loads[7].wait()

    for k in range(EQ):
        column = mask_in[:, k : k + 1].astype(F32)
        mask_cols[EQ * k : EQ * k + EQ, :] = jnp.broadcast_to(column, (EQ, LANES))

    def west_on(j):
        code = codes[rows(j, 1), :]
        return jnp.where((code == 0) | (code == 1), 1.0, 0.0).astype(F32)

    def east_on(j):
        code = codes[rows(j, 1), :]
        return jnp.where((code == 0) | (code == 2), 1.0, 0.0).astype(F32)

    send_edge_maps()
    a_all[0:EQ, :] = jnp.zeros((EQ, LANES), F32)
    b_all[(WALL - 1) * EQ : WALL * EQ, :] = jnp.zeros((EQ, LANES), F32)

    def halo_copy(sweep, side, other):
        return pltpu.make_async_remote_copy(
            src_ref=halo_out.at[sweep, side],
            dst_ref=halo_in.at[sweep, side],
            send_sem=halo_send.at[sweep, side],
            recv_sem=halo_recv.at[sweep, side],
            device_id={"stream": other},
            device_id_type=MESH,
        )

    def source_cell(j):
        block = jnp.minimum(j, CELLS - 1)
        base = pl.multiple_of(block * BLOCK, BLOCK)
        at = pl.multiple_of(block * EQ, EQ)
        s_rows[rows(pl.multiple_of(j * EQ, EQ), EQ), :] = (
            rhs[block] - times(west, base, uw_rows, at) - times(east, base, ue_rows, at)
        )

    maps_b, maps_d = WALL * BLOCK, 2 * WALL * BLOCK

    def rise():
        a_all[EQ : 2 * EQ, :] = q_all[0:EQ, :]
        for i in range(1, WALL):
            part = slice(EQ * i, EQ * i + EQ)
            if i < WALL - 1:
                a_all[EQ * i + EQ : EQ * i + 2 * EQ, :] = q_all[part, :] + times(
                    others, BLOCK * i, a_all, EQ * i
                )
            total = r_all[part, :] + times(others, maps_b + BLOCK * i, a_all, EQ * i)
            if i < WALL - 1:
                r_all[part, :] = total
            else:
                b_all[EQ * i - EQ : EQ * i, :] = total

    lax.fori_loop(0, 2, take_map, 0)
    take_up()
    rise()
    take_map(2, 0)

    def one_sweep(sweep, carry):
        for step in range(1, WALL - 1):
            i = WALL - 1 - step
            b_all[EQ * i - EQ : EQ * i, :] = r_all[EQ * i : EQ * i + EQ, :] + times(
                others, maps_d + BLOCK * i, b_all, EQ * i
            )
        send_back(sweep)

        @pl.when(sweep < SWEEPS - 1)
        def _():
            pair = pack_edges([r_rows[EQ * j : EQ * j + EQ, :] for j in range(CELLS)])
            for side, other in ((0, next_stream), (1, last_stream)):
                halo_out[sweep, side] = pair[side]
                halo_copy(sweep, side, other).start()

        @pl.when(sweep == 0)
        def _():
            loads[4].wait()
            by_columns(west_in, west, west_on)
            loads[5].wait()
            by_columns(east_in, east, east_on)
            take_edge_maps()

        take_back()
        on_ghosts(sweep, lambda copy: copy.wait_send())

        def update_cell(j, carry):
            base = pl.multiple_of(j * BLOCK, BLOCK)
            at = pl.multiple_of(j * EQ, EQ)
            out[j] = (
                r_rows[rows(at, EQ), :]
                + times(b_maps, base, ab_rows, 0)
                + times(d_maps, base, ab_rows, EQ)
            )
            return carry

        lax.fori_loop(0, CELLS, update_cell, 0)

        @pl.when(sweep < SWEEPS - 1)
        def _():
            for j in range(CELLS):
                uw_rows[EQ * j : EQ * j + EQ, :] = pltpu.roll(out[j], 1, 1)
                ue_rows[EQ * j : EQ * j + EQ, :] = pltpu.roll(out[j], LANES - 1, 1)
            for side, other in ((0, next_stream), (1, last_stream)):
                halo_copy(sweep, side, other).wait()
            for side in range(2):
                pltpu.make_async_remote_copy(
                    src_ref=back_out.at[0],
                    dst_ref=ghost_in.at[sweep, side],
                    send_sem=ghost_send.at[sweep, 0],
                    recv_sem=ghost_recv.at[sweep, side],
                    device_id={"stream": next_stream},
                    device_id_type=MESH,
                ).wait_recv()
            from_west, from_east = ghost_in[sweep, 0], ghost_in[sweep, 1]
            for v in range(SIDE):
                ghost_ab[8 * v : 8 * v + 8, :] = jnp.where(
                    lane < 8,
                    jnp.broadcast_to(from_west[:, 32 * v + 31 : 32 * v + 32], (8, LANES)),
                    jnp.broadcast_to(from_east[:, 32 * v : 32 * v + 1], (8, LANES)),
                )
            ghosts = (
                jnp.where(lane16 < 8, halo_in[sweep, 0], halo_in[sweep, 1])
                + times(b_edge, 0, ghost_ab, 0)
                + times(d_edge, 0, ghost_ab, EQ)
            )
            west_ghosts = jnp.where(stream == 0, 0.0, ghosts)
            east_ghosts = jnp.where(stream == streams - 1, 0.0, ghosts)
            for j in range(CELLS):
                part = slice(EQ * j, EQ * j + EQ)
                ghost = pltpu.roll(west_ghosts, LANES - j, 1) if j else west_ghosts
                uw_rows[part, :] = jnp.where(lane16 == 0, ghost, uw_rows[part, :])
                ghost = pltpu.roll(east_ghosts, LANES - 9 - j, 1)
                ue_rows[part, :] = jnp.where(lane16 == LANES - 1, ghost, ue_rows[part, :])

            source_cell(0)
            source_cell(1)
            forward_cell(0)
            q_rows[0:EQ, :] = f_rows[0:EQ, :]
            source_cell(2)
            forward_cell(1)

            def next_up(j, carry):
                up_cell(j)
                forward_cell(j + 1)
                source_cell(j + 2)
                return carry

            lax.fori_loop(1, CELLS, next_up, 0)
            down_chain()
            send_up()
            take_up()
            rise()

        return carry

    lax.fori_loop(0, SWEEPS, one_sweep, 0)


def on_device(*arrays):
    big = pltpu.VMEM((CELLS * BLOCK, LANES), F32)
    block = pltpu.VMEM((BLOCK, LANES), F32)
    vectors = pltpu.VMEM((CELLS * EQ, LANES), F32)
    padded = pltpu.VMEM(((CELLS + 2) * EQ, LANES), F32)
    pair = pltpu.VMEM((2 * EQ, LANES), F32)
    wall = pltpu.VMEM((WALL * EQ, LANES), F32)
    narrow = pltpu.VMEM((CELLS, EQ, EQ, LANES), jnp.bfloat16)
    tiles = pltpu.VMEM((WALL, 8, LANES), F32)
    return pl.pallas_call(
        kernel,
        out_shape=jax.ShapeDtypeStruct((CELLS, EQ, LANES), F32),
        in_specs=[pl.BlockSpec(memory_space=pltpu.HBM)] * 8,
        out_specs=pl.BlockSpec(memory_space=pltpu.VMEM),
        scratch_shapes=[
            pltpu.VMEM((CELLS, EQ, LANES), F32), narrow, narrow, narrow, narrow, narrow,
            pltpu.VMEM((EQ, EQ), jnp.int32), pltpu.VMEM((CELLS, LANES), jnp.int32),
            big, block, big, big, big, big, big, big, big, big,
            pltpu.VMEM((3 * WALL * BLOCK, LANES), F32),
            padded, vectors, vectors, vectors, vectors, padded, pair,
            wall, wall, wall, wall,
            pltpu.VMEM((3, WALL, EQ, LANES), F32),
            pltpu.VMEM((3, WALL, EQ, LANES), F32),
            pltpu.VMEM((SIDE, 8, LANES), F32), tiles, tiles, tiles,
            pltpu.VMEM((SWEEPS - 1, 2, EQ, LANES), F32),
            pltpu.VMEM((SWEEPS - 1, 2, EQ, LANES), F32),
            pltpu.VMEM((2, 2, BLOCK, LANES), F32),
            pltpu.VMEM((2, 2, BLOCK, LANES), F32),
            block, block,
            pltpu.VMEM((SWEEPS - 1, 2, 8, LANES), F32),
            pair,
            pltpu.SemaphoreType.DMA((8,)),
            pltpu.SemaphoreType.DMA((3, WALL)),
            pltpu.SemaphoreType.DMA((3, WALL)),
            pltpu.SemaphoreType.DMA((2, WALL)),
            pltpu.SemaphoreType.DMA((2, WALL)),
            pltpu.SemaphoreType.DMA((SWEEPS - 1, 2)),
            pltpu.SemaphoreType.DMA((SWEEPS - 1, 2)),
            pltpu.SemaphoreType.DMA((2,)),
            pltpu.SemaphoreType.DMA((2,)),
            pltpu.SemaphoreType.DMA((SWEEPS - 1, WALL)),
            pltpu.SemaphoreType.DMA((SWEEPS - 1, 2)),
            pltpu.SemaphoreType.REGULAR,
        ],
        compiler_params=pltpu.CompilerParams(collective_id=0, has_side_effects=True),
    )(*arrays)


def solution(mesh):
    return jax.shard_map(
        on_device,
        mesh=mesh,
        in_specs=(
            P("wall", None, "stream"),
            P("wall", None, None, "stream"),
            P("wall", None, None, "stream"),
            P("wall", None, None, "stream"),
            P("wall", None, None, "stream"),
            P("wall", None, None, "stream"),
            P(),
            P("wall", "stream"),
        ),
        out_specs=P("wall", None, "stream"),
        check_vma=False,
    )
```

```python
import jax
import jax.numpy as jnp
from jax import lax
from jax.experimental import pallas as pl
from jax.experimental.pallas import tpu as pltpu
from jax.sharding import PartitionSpec as P

SWEEPS = 3
EQ = 16
CELLS = 8
LANES = 128
WALL = 16
SIDE = 4
BLOCK = EQ * EQ
MESH = pl.DeviceIdType.MESH
F32 = jnp.float32

OFFSETS = sorted(
    [(dy, dx) for dy in range(SIDE) for dx in range(SIDE) if dy or dx],
    key=lambda o: -(min(o[0], SIDE - o[0]) + min(o[1], SIDE - o[1])),
)


def rows(start, size):
    return pl.ds(start, size)


def tree_sum(parts):
    while len(parts) > 1:
        parts = [
            parts[k] + parts[k + 1] if k + 1 < len(parts) else parts[k]
            for k in range(0, len(parts), 2)
        ]
    return parts[0]


def times(blocks, base, vectors, at):
    return tree_sum(
        [
            blocks[rows(base + EQ * k, EQ), :] * vectors[rows(at + k, 1), :]
            for k in range(EQ)
        ]
    )


def block_product(out, out_base, left, left_base, right, right_base, add=None, add_base=0):
    for first in range(0, BLOCK, 4 * EQ):
        sums = [None] * 4
        if add is not None:
            sums = [add[rows(add_base + first + EQ * m, EQ), :] for m in range(4)]
        for k in range(EQ):
            column = left[rows(left_base + EQ * k, EQ), :]
            for m in range(4):
                term = column * right[rows(right_base + first + EQ * m + k, 1), :]
                sums[m] = term if sums[m] is None else sums[m] + term
        for m in range(4):
            out[rows(out_base + first + EQ * m, EQ), :] = sums[m]


def swap_four(values, slot, width):
    moved = []
    for u in range(SIDE):
        total = None
        for v in range(SIDE):
            piece = values[v] if u == v else pltpu.roll(values[v], (width * (v - u)) % LANES, 1)
            total = piece if total is None else jnp.where(slot == v, piece, total)
        moved.append(total)
    return moved


def kernel(
    rhs_hbm, pivot_hbm, lower_hbm, upper_hbm, west_hbm, east_hbm, mask_hbm, codes_hbm, out,
    rhs, pivot_in, lower_in, upper_in, west_in, east_in, mask_in, codes,
    temp, mask_cols, pivot, lower, upper, west, east, c_maps, d_maps, b_maps, others,
    f_rows, q_rows, r_rows, uw_rows, ue_rows, s_rows, ab_rows,
    q_all, r_all, a_all, b_all,
    map_out, map_in, up_out, up_in, back_out, back_in, halo_out, halo_in,
    edge_out, edge_in, b_edge, d_edge, ghost_in, ghost_ab,
    load_sem, map_send, map_recv, vec_send, vec_recv, halo_send, halo_recv,
    edge_send, edge_recv, ghost_send, ghost_recv, ready,
):
    me = lax.axis_index("wall")
    stream = lax.axis_index("stream")
    streams = lax.axis_size("stream")
    my_y, my_x = me // SIDE, me % SIDE
    peers = [((my_y + dy) % SIDE) * SIDE + (my_x + dx) % SIDE for dy, dx in OFFSETS]
    next_stream = lax.rem(stream + 1, streams)
    last_stream = lax.rem(stream + streams - 1, streams)
    sends = (stream < streams - 1, stream > 0)
    takes = (stream > 0, stream < streams - 1)
    lane = lax.broadcasted_iota(jnp.int32, (8, LANES), 1)
    lane16 = lax.broadcasted_iota(jnp.int32, (EQ, LANES), 1)
    high_slot, low_slot = lane // 32, (lane // 8) % SIDE

    loads = [
        pltpu.make_async_copy(source, target, load_sem.at[k])
        for k, (source, target) in enumerate(
            [
                (lower_hbm, lower_in),
                (upper_hbm, upper_in),
                (pivot_hbm, pivot_in),
                (rhs_hbm, rhs),
                (west_hbm, west_in),
                (east_hbm, east_in),
                (mask_hbm, mask_in),
                (codes_hbm, codes),
            ]
        )
    ]
    for load in loads:
        load.start()

    barrier = pltpu.get_barrier_semaphore()
    for peer in peers:
        pl.semaphore_signal(barrier, inc=1, device_id={"wall": peer}, device_id_type=MESH)
    for other in (next_stream, last_stream):
        pl.semaphore_signal(barrier, inc=1, device_id={"stream": other}, device_id_type=MESH)

    def column_cell(j, source, target, scale=None):
        base = pl.multiple_of(j * BLOCK, BLOCK)
        for c in range(EQ):
            temp[rows(base + EQ * c, EQ), :] = source[j, c].astype(F32)
        factor = None if scale is None else scale(j)
        for k in range(EQ):
            column = temp[pl.ds(base + k, EQ, stride=EQ), :]
            if factor is not None:
                column = column * (mask_cols[EQ * k : EQ * k + EQ, :] * factor)
            target[rows(base + EQ * k, EQ), :] = column

    def by_columns(source, target, scale=None):
        def one_cell(j, carry):
            column_cell(j, source, target, scale)
            return carry

        lax.fori_loop(0, CELLS, one_cell, 0)

    def map_copy(which, peer):
        return pltpu.make_async_remote_copy(
            src_ref=map_out.at[which, peer],
            dst_ref=map_in.at[which, me],
            send_sem=map_send.at[which, peer],
            recv_sem=map_recv.at[which, me],
            device_id={"wall": peer},
            device_id_type=MESH,
        )

    def map_arrival(which, peer):
        return pltpu.make_async_remote_copy(
            src_ref=map_out.at[which, peer],
            dst_ref=map_in.at[which, peer],
            send_sem=map_send.at[which, peer],
            recv_sem=map_recv.at[which, peer],
            device_id={"wall": peer},
            device_id_type=MESH,
        )

    def send_map(which, maps, base):
        for half in range(2):
            grid = [
                [maps[rows(base + EQ * (SIDE * high + low) + 8 * half, 8), :] for high in range(SIDE)]
                for low in range(SIDE)
            ]
            grid = [swap_four(values, high_slot, 32) for values in grid]
            for high in range(SIDE):
                values = swap_four([grid[low][high] for low in range(SIDE)], low_slot, 8)
                for low, value in enumerate(values):
                    map_out[which, SIDE * high + low, 8 * half : 8 * half + 8, :] = value
        for peer in peers:
            map_copy(which, peer).start()
        map_in[which, me] = map_out[which, me]

    def take_map(which, carry):
        for peer in peers:
            map_arrival(which, peer).wait_recv()
        for peer in peers:
            map_copy(which, peer).wait_send()
        shifts = [(8 * (my_x - m) + LANES) % LANES for m in range(EQ)]
        for i in range(WALL):
            value = map_in[which, i]
            for m in range(EQ):
                at = pl.multiple_of(which * (WALL * BLOCK) + BLOCK * i + EQ * m, EQ)
                others[rows(at, EQ), :] = pltpu.roll(value, shifts[m], 1)
        return carry

    loads[0].wait()
    by_columns(lower_in, lower)
    loads[1].wait()
    column_cell(0, upper_in, upper)
    c_maps[0:BLOCK, :] = lower[0:BLOCK, :]

    def c_cell(j, carry):
        base = pl.multiple_of(j * BLOCK, BLOCK)
        block_product(c_maps, base, lower, base, c_maps, base - BLOCK)
        column_cell(j, upper_in, upper)
        return carry

    lax.fori_loop(1, CELLS, c_cell, 0)
    pl.semaphore_wait(barrier, len(peers) + 2)

    for owner in (WALL - 1, 0):

        @pl.when(me != owner)
        def _():
            pl.semaphore_signal(ready, inc=1, device_id={"wall": owner}, device_id_type=MESH)

    send_map(0, c_maps, (CELLS - 1) * BLOCK)

    loads[2].wait()
    column_cell(0, pivot_in, pivot)
    d_maps[(CELLS - 1) * BLOCK : CELLS * BLOCK, :] = upper[(CELLS - 1) * BLOCK : CELLS * BLOCK, :]
    final = (CELLS - 1) * BLOCK
    b_maps[final : final + BLOCK, :] = c_maps[final : final + BLOCK, :]

    def b_cell(step, carry):
        base = pl.multiple_of((CELLS - 1 - step) * BLOCK, BLOCK)
        block_product(b_maps, base, upper, base, b_maps, base + BLOCK, c_maps, base)
        column_cell(step, pivot_in, pivot)
        return carry

    lax.fori_loop(1, CELLS, b_cell, 0)
    send_map(1, b_maps, 0)

    def forward_cell(j):
        block = jnp.minimum(j, CELLS - 1)
        base = pl.multiple_of(block * BLOCK, BLOCK)
        at = pl.multiple_of(j * EQ, EQ)
        f_rows[rows(at, EQ), :] = times(pivot, base, s_rows, at)

    def up_cell(j):
        base = pl.multiple_of(j * BLOCK, BLOCK)
        at = pl.multiple_of(j * EQ, EQ)
        q_rows[rows(at, EQ), :] = f_rows[rows(at, EQ), :] + times(lower, base, q_rows, at - EQ)

    def down_chain():
        last = (CELLS - 1) * EQ
        r_rows[last : last + EQ, :] = q_rows[last : last + EQ, :]

        def down(step, carry):
            j = CELLS - 1 - step
            base = pl.multiple_of(j * BLOCK, BLOCK)
            at = pl.multiple_of(j * EQ, EQ)
            r_rows[rows(at, EQ), :] = q_rows[rows(at, EQ), :] + times(upper, base, r_rows, at + EQ)
            return carry

        lax.fori_loop(1, CELLS, down, 0)

    def up_copy(peer):
        return pltpu.make_async_remote_copy(
            src_ref=up_out.at[peer // SIDE],
            dst_ref=up_in.at[me],
            send_sem=vec_send.at[0, peer],
            recv_sem=vec_recv.at[0, me],
            device_id={"wall": peer},
            device_id_type=MESH,
        )

    def up_arrival(peer):
        return pltpu.make_async_remote_copy(
            src_ref=up_out.at[0],
            dst_ref=up_in.at[peer],
            send_sem=vec_send.at[0, peer],
            recv_sem=vec_recv.at[0, peer],
            device_id={"wall": peer},
            device_id_type=MESH,
        )

    def back_copy(peer):
        return pltpu.make_async_remote_copy(
            src_ref=back_out.at[peer],
            dst_ref=back_in.at[me],
            send_sem=vec_send.at[1, peer],
            recv_sem=vec_recv.at[1, me],
            device_id={"wall": peer},
            device_id_type=MESH,
        )

    def back_arrival(peer):
        return pltpu.make_async_remote_copy(
            src_ref=back_out.at[peer],
            dst_ref=back_in.at[peer],
            send_sem=vec_send.at[1, peer],
            recv_sem=vec_recv.at[1, peer],
            device_id={"wall": peer},
            device_id_type=MESH,
        )

    def send_up():
        top = (CELLS - 1) * EQ
        values = [
            q_rows[top : top + 8, :],
            q_rows[top + 8 : top + 16, :],
            r_rows[0:8, :],
            r_rows[8:16, :],
        ]
        for u, value in enumerate(swap_four(values, high_slot, 32)):
            up_out[u] = value
        for peer in peers:
            up_copy(peer).start()
        up_in[me] = up_out[my_y]

    def take_up():
        for peer in peers:
            up_arrival(peer).wait_recv()
        for peer in peers:
            up_copy(peer).wait_send()
        for i in range(WALL):
            tile = up_in[i]
            q_all[EQ * i : EQ * i + 8, :] = tile
            q_all[EQ * i + 8 : EQ * i + 16, :] = pltpu.roll(tile, LANES - 32, 1)
            r_all[EQ * i : EQ * i + 8, :] = pltpu.roll(tile, LANES - 64, 1)
            r_all[EQ * i + 8 : EQ * i + 16, :] = pltpu.roll(tile, LANES - 96, 1)

    def ghost_copy(sweep, side, i):
        return pltpu.make_async_remote_copy(
            src_ref=back_out.at[i],
            dst_ref=ghost_in.at[sweep, side],
            send_sem=ghost_send.at[sweep, i],
            recv_sem=ghost_recv.at[sweep, side],
            device_id={"wall": i, "stream": last_stream if side else next_stream},
            device_id_type=MESH,
        )

    def on_ghosts(sweep, act):
        for side, owner in ((0, WALL - 1), (1, 0)):

            @pl.when((sweep < SWEEPS - 1) & (me == owner) & sends[side])
            def _():
                for i in range(WALL):
                    act(ghost_copy(sweep, side, i))

    def pack_edges(values):
        to_next, to_last = None, None
        for j, value in enumerate(values):
            high, low = pltpu.roll(value, j + 1, 1), pltpu.roll(value, 8 + j, 1)
            to_next = high if j == 0 else jnp.where(lane16 == j, high, to_next)
            to_last = low if j == 0 else jnp.where(lane16 == 8 + j, low, to_last)
        return to_next, to_last

    def edge_copy(side, other):
        return pltpu.make_async_remote_copy(
            src_ref=edge_out.at[side],
            dst_ref=edge_in.at[side],
            send_sem=edge_send.at[side],
            recv_sem=edge_recv.at[side],
            device_id={"stream": other},
            device_id_type=MESH,
        )

    def send_edge_maps():
        def some_columns(step, carry):
            for m in range(8):
                at = pl.multiple_of(step * (8 * EQ) + EQ * m, EQ)
                for which, maps in enumerate((b_maps, d_maps)):
                    pair = pack_edges([maps[rows(BLOCK * j + at, EQ), :] for j in range(CELLS)])
                    for side in range(2):
                        edge_out[side, which, rows(at, EQ), :] = pair[side]
            return carry

        lax.fori_loop(0, 2, some_columns, 0)
        for side, other in ((0, next_stream), (1, last_stream)):
            pl.when(sends[side])(edge_copy(side, other).start)

    def take_edge_maps():
        for side, other in ((0, next_stream), (1, last_stream)):
            pl.when(sends[side])(edge_copy(side, other).wait_send)
            pl.when(takes[side])(edge_copy(side, other).wait_recv)
        for m in range(EQ):
            part = slice(EQ * m, EQ * m + EQ)
            for which, maps in enumerate((b_edge, d_edge)):
                maps[part, :] = jnp.where(
                    lane16 < 8, edge_in[0, which, part, :], edge_in[1, which, part, :]
                )

    def send_back(sweep):
        for i in range(WALL):
            tile = a_all[EQ * i : EQ * i + 8, :]
            for v, piece in enumerate(
                [
                    a_all[EQ * i + 8 : EQ * i + 16, :],
                    b_all[EQ * i : EQ * i + 8, :],
                    b_all[EQ * i + 8 : EQ * i + 16, :],
                ]
            ):
                tile = jnp.where(high_slot == v + 1, pltpu.roll(piece, 32 * (v + 1), 1), tile)
            back_out[i] = tile

        @pl.when((sweep == 0) & (me % (WALL - 1) == 0))
        def _():
            pl.semaphore_wait(ready, WALL - 1)

        on_ghosts(sweep, lambda copy: copy.start())
        for peer in peers:
            back_copy(peer).start()
        back_in[me] = back_out[me]

    def take_back():
        for peer in peers:
            back_arrival(peer).wait_recv()
        for peer in peers:
            back_copy(peer).wait_send()
        values = []
        for high in range(SIDE):
            total = back_in[SIDE * high]
            for low in range(1, SIDE):
                total = jnp.where(low_slot == low, back_in[SIDE * high + low], total)
            values.append(total)
        for v, value in enumerate(swap_four(values, high_slot, 32)):
            ab_rows[8 * v : 8 * v + 8, :] = value

    loads[3].wait()
    for j in range(CELLS):
        s_rows[EQ * j : EQ * j + EQ, :] = rhs[j]
    forward_cell(0)
    q_rows[0:EQ, :] = f_rows[0:EQ, :]
    forward_cell(1)

    def first_up(j, carry):
        up_cell(j)
        forward_cell(j + 1)
        return carry

    lax.fori_loop(1, CELLS, first_up, 0)
    down_chain()
    send_up()

    def d_cell(step, carry):
        base = pl.multiple_of((CELLS - 1 - step) * BLOCK, BLOCK)
        block_product(d_maps, base, upper, base, d_maps, base + BLOCK)
        return carry

    lax.fori_loop(1, CELLS, d_cell, 0)
    send_map(2, d_maps, 0)

    loads[6].wait()
    loads[7].wait()

    for k in range(EQ):
        column = mask_in[:, k : k + 1].astype(F32)
        mask_cols[EQ * k : EQ * k + EQ, :] = jnp.broadcast_to(column, (EQ, LANES))

    def west_on(j):
        code = codes[rows(j, 1), :]
        return jnp.where((code == 0) | (code == 1), 1.0, 0.0).astype(F32)

    def east_on(j):
        code = codes[rows(j, 1), :]
        return jnp.where((code == 0) | (code == 2), 1.0, 0.0).astype(F32)

    send_edge_maps()
    a_all[0:EQ, :] = jnp.zeros((EQ, LANES), F32)
    b_all[(WALL - 1) * EQ : WALL * EQ, :] = jnp.zeros((EQ, LANES), F32)

    def halo_copy(sweep, side, other):
        return pltpu.make_async_remote_copy(
            src_ref=halo_out.at[sweep, side],
            dst_ref=halo_in.at[sweep, side],
            send_sem=halo_send.at[sweep, side],
            recv_sem=halo_recv.at[sweep, side],
            device_id={"stream": other},
            device_id_type=MESH,
        )

    def source_cell(j):
        block = jnp.minimum(j, CELLS - 1)
        base = pl.multiple_of(block * BLOCK, BLOCK)
        at = pl.multiple_of(block * EQ, EQ)
        s_rows[rows(pl.multiple_of(j * EQ, EQ), EQ), :] = (
            rhs[block] - times(west, base, uw_rows, at) - times(east, base, ue_rows, at)
        )

    maps_b, maps_d = WALL * BLOCK, 2 * WALL * BLOCK

    def rise():
        a_all[EQ : 2 * EQ, :] = q_all[0:EQ, :]
        for i in range(1, WALL):
            part = slice(EQ * i, EQ * i + EQ)
            if i < WALL - 1:
                a_all[EQ * i + EQ : EQ * i + 2 * EQ, :] = q_all[part, :] + times(
                    others, BLOCK * i, a_all, EQ * i
                )
            total = r_all[part, :] + times(others, maps_b + BLOCK * i, a_all, EQ * i)
            if i < WALL - 1:
                r_all[part, :] = total
            else:
                b_all[EQ * i - EQ : EQ * i, :] = total

    lax.fori_loop(0, 2, take_map, 0)
    take_up()
    rise()
    take_map(2, 0)

    def one_sweep(sweep, carry):
        for step in range(1, WALL - 1):
            i = WALL - 1 - step
            b_all[EQ * i - EQ : EQ * i, :] = r_all[EQ * i : EQ * i + EQ, :] + times(
                others, maps_d + BLOCK * i, b_all, EQ * i
            )
        send_back(sweep)

        @pl.when(sweep < SWEEPS - 1)
        def _():
            pair = pack_edges([r_rows[EQ * j : EQ * j + EQ, :] for j in range(CELLS)])
            for side, other in ((0, next_stream), (1, last_stream)):
                halo_out[sweep, side] = pair[side]
                pl.when(sends[side])(halo_copy(sweep, side, other).start)

        @pl.when(sweep == 0)
        def _():
            loads[4].wait()
            by_columns(west_in, west, west_on)
            loads[5].wait()
            by_columns(east_in, east, east_on)
            take_edge_maps()

        take_back()
        on_ghosts(sweep, lambda copy: copy.wait_send())

        def update_cell(j, carry):
            base = pl.multiple_of(j * BLOCK, BLOCK)
            at = pl.multiple_of(j * EQ, EQ)
            out[j] = (
                r_rows[rows(at, EQ), :]
                + times(b_maps, base, ab_rows, 0)
                + times(d_maps, base, ab_rows, EQ)
            )
            return carry

        lax.fori_loop(0, CELLS, update_cell, 0)

        @pl.when(sweep < SWEEPS - 1)
        def _():
            for j in range(CELLS):
                uw_rows[EQ * j : EQ * j + EQ, :] = pltpu.roll(out[j], 1, 1)
                ue_rows[EQ * j : EQ * j + EQ, :] = pltpu.roll(out[j], LANES - 1, 1)
            for side, other in ((0, next_stream), (1, last_stream)):
                pl.when(sends[side])(halo_copy(sweep, side, other).wait_send)
                pl.when(takes[side])(halo_copy(sweep, side, other).wait_recv)
            for side in range(2):
                arrival = pltpu.make_async_remote_copy(
                    src_ref=back_out.at[0],
                    dst_ref=ghost_in.at[sweep, side],
                    send_sem=ghost_send.at[sweep, 0],
                    recv_sem=ghost_recv.at[sweep, side],
                    device_id={"stream": next_stream},
                    device_id_type=MESH,
                )
                pl.when(takes[side])(arrival.wait_recv)
            from_west, from_east = ghost_in[sweep, 0], ghost_in[sweep, 1]
            for v in range(SIDE):
                ghost_ab[8 * v : 8 * v + 8, :] = jnp.where(
                    lane < 8,
                    jnp.broadcast_to(from_west[:, 32 * v + 31 : 32 * v + 32], (8, LANES)),
                    jnp.broadcast_to(from_east[:, 32 * v : 32 * v + 1], (8, LANES)),
                )
            ghosts = (
                jnp.where(lane16 < 8, halo_in[sweep, 0], halo_in[sweep, 1])
                + times(b_edge, 0, ghost_ab, 0)
                + times(d_edge, 0, ghost_ab, EQ)
            )
            west_ghosts = jnp.where(stream == 0, 0.0, ghosts)
            east_ghosts = jnp.where(stream == streams - 1, 0.0, ghosts)
            for j in range(CELLS):
                part = slice(EQ * j, EQ * j + EQ)
                ghost = pltpu.roll(west_ghosts, LANES - j, 1) if j else west_ghosts
                uw_rows[part, :] = jnp.where(lane16 == 0, ghost, uw_rows[part, :])
                ghost = pltpu.roll(east_ghosts, LANES - 9 - j, 1)
                ue_rows[part, :] = jnp.where(lane16 == LANES - 1, ghost, ue_rows[part, :])

            source_cell(0)
            source_cell(1)
            forward_cell(0)
            q_rows[0:EQ, :] = f_rows[0:EQ, :]
            source_cell(2)
            forward_cell(1)

            def next_up(j, carry):
                up_cell(j)
                forward_cell(j + 1)
                source_cell(j + 2)
                return carry

            lax.fori_loop(1, CELLS, next_up, 0)
            down_chain()
            send_up()
            take_up()
            rise()

        return carry

    lax.fori_loop(0, SWEEPS, one_sweep, 0)


def on_device(*arrays):
    big = pltpu.VMEM((CELLS * BLOCK, LANES), F32)
    block = pltpu.VMEM((BLOCK, LANES), F32)
    vectors = pltpu.VMEM((CELLS * EQ, LANES), F32)
    padded = pltpu.VMEM(((CELLS + 2) * EQ, LANES), F32)
    pair = pltpu.VMEM((2 * EQ, LANES), F32)
    wall = pltpu.VMEM((WALL * EQ, LANES), F32)
    narrow = pltpu.VMEM((CELLS, EQ, EQ, LANES), jnp.bfloat16)
    tiles = pltpu.VMEM((WALL, 8, LANES), F32)
    return pl.pallas_call(
        kernel,
        out_shape=jax.ShapeDtypeStruct((CELLS, EQ, LANES), F32),
        in_specs=[pl.BlockSpec(memory_space=pltpu.HBM)] * 8,
        out_specs=pl.BlockSpec(memory_space=pltpu.VMEM),
        scratch_shapes=[
            pltpu.VMEM((CELLS, EQ, LANES), F32), narrow, narrow, narrow, narrow, narrow,
            pltpu.VMEM((EQ, EQ), jnp.int32), pltpu.VMEM((CELLS, LANES), jnp.int32),
            big, block, big, big, big, big, big, big, big, big,
            pltpu.VMEM((3 * WALL * BLOCK, LANES), F32),
            padded, vectors, vectors, vectors, vectors, padded, pair,
            wall, wall, wall, wall,
            pltpu.VMEM((3, WALL, EQ, LANES), F32),
            pltpu.VMEM((3, WALL, EQ, LANES), F32),
            pltpu.VMEM((SIDE, 8, LANES), F32), tiles, tiles, tiles,
            pltpu.VMEM((SWEEPS - 1, 2, EQ, LANES), F32),
            pltpu.VMEM((SWEEPS - 1, 2, EQ, LANES), F32),
            pltpu.VMEM((2, 2, BLOCK, LANES), F32),
            pltpu.VMEM((2, 2, BLOCK, LANES), F32),
            block, block,
            pltpu.VMEM((SWEEPS - 1, 2, 8, LANES), F32),
            pair,
            pltpu.SemaphoreType.DMA((8,)),
            pltpu.SemaphoreType.DMA((3, WALL)),
            pltpu.SemaphoreType.DMA((3, WALL)),
            pltpu.SemaphoreType.DMA((2, WALL)),
            pltpu.SemaphoreType.DMA((2, WALL)),
            pltpu.SemaphoreType.DMA((SWEEPS - 1, 2)),
            pltpu.SemaphoreType.DMA((SWEEPS - 1, 2)),
            pltpu.SemaphoreType.DMA((2,)),
            pltpu.SemaphoreType.DMA((2,)),
            pltpu.SemaphoreType.DMA((SWEEPS - 1, WALL)),
            pltpu.SemaphoreType.DMA((SWEEPS - 1, 2)),
            pltpu.SemaphoreType.REGULAR,
        ],
        compiler_params=pltpu.CompilerParams(collective_id=0, has_side_effects=True),
    )(*arrays)


def solution(mesh):
    return jax.shard_map(
        on_device,
        mesh=mesh,
        in_specs=(
            P("wall", None, "stream"),
            P("wall", None, None, "stream"),
            P("wall", None, None, "stream"),
            P("wall", None, None, "stream"),
            P("wall", None, None, "stream"),
            P("wall", None, None, "stream"),
            P(),
            P("wall", "stream"),
        ),
        out_specs=P("wall", None, "stream"),
        check_vma=False,
    )
```
